32 devices in a mesh: groups: 2 (over y), blk: 4 (over z), dp: 2 (over x), sub: 2 (over core).
Axes of the slice: x: 2, y: 2, z: 4, core: 2. Of those that a mesh axis runs over, the one named last changes fastest.
Arguments:
- view_a: bfloat16 [2048, 256], P(('groups', 'blk', 'dp', 'sub')), parts along dimension 0, may hold values from -6 to 6
- view_b: bfloat16 [2048, 256], P(('groups', 'blk', 'dp', 'sub')), parts along dimension 0, may hold values from -6 to 6
- prototypes: bfloat16 [32768, 256], P('blk'), may hold values from -6 to 6
- tile_mask: int32 [16, 256], replicated, may hold values from 0 to 1, as said below
- tile_region: int32 [32], P('groups'), parts along dimension 0, may hold values from 0 to 15, as said below
Outputs:
- grad_view_b: float32 [2048, 256], P(('groups', 'blk', 'dp', 'sub')), parts along dimension 0
- grad_prototypes: float32 [65536, 256], P(('groups', 'blk', 'dp', 'sub')), parts along dimension 0
The draws below stay inside these ranges and needn't reach their ends.
There are 2 independent parts, one for each index of `groups`. The reference program is written for one: setup_inputs(seed, part) draws one part's arguments, and reference() takes and returns one part's arrays. A program takes and returns all parts, laid end to end along the dimension named above; an argument that names none is the same for every part. Nothing has to cross between parts.
Inputs may be any that keep to these rules, and one draw needn't show every extreme that they name: `tile_mask`: every prototype tile is 1 for at least one region, and every region for at least 16 tiles. `tile_region`: every region is named by at least one hit tile.
All inputs are finite; a program needn't handle non-finite values.
Results may differ from the reference program's by a relative error of at most 0.00045.
The reference program's roundings to bfloat16 on the way count: a program that leaves them out, or rounds other values in their place, can miss the bound.
Values may be sent and summed in bfloat16 or wider, within the bound.
A program may use at most 64 MiB of HBM per device.

```python
import jax
import jax.numpy as jnp
from jax import lax

D = 256
K = 32768
TILE = 128
REGIONS = 16
ITERS = 3
HIT_DEV = 64
HIT_TILES = 16
HITS = 1024
KT = 256


def draw_tile_mask(key, part):
    first_key, second_key = jax.random.split(key)
    shuffled = jax.random.permutation(first_key, KT)
    homes = shuffled % REGIONS
    region_ids = jnp.arange(REGIONS, dtype=jnp.int32)
    home_flags = homes[None, :] == region_ids[:, None]
    extra_bits = jax.random.randint(second_key, (REGIONS, KT), 0, 4) == 0
    return jnp.logical_or(home_flags, extra_bits).astype(jnp.int32)


def draw_tile_region(key, part):
    shuffled = jax.random.permutation(key, HIT_TILES)
    return (shuffled % REGIONS).astype(jnp.int32)


def block_scale(key, extent, cuts, smallest, top_value):
    def one(position, shards_of):
        draws = jax.random.uniform(jax.random.fold_in(jax.random.fold_in(key, 6), position), (shards_of,), jnp.float32, smallest / len(cuts), top_value / len(cuts))
        return jnp.repeat(jnp.exp(draws), extent[position] // shards_of).reshape((-1,) + (1,) * (len(extent) - position - 1))

    gain = one(*cuts[0])
    for cut in cuts[1:]:
        gain = gain * one(*cut)
    return gain


def normal_values(key, shape, width, reach, cuts=(), held_as=jnp.bfloat16):
    gain = block_scale(key, shape, cuts, -0.22, 0.18) if cuts else 1.0
    values = jax.random.normal(key, shape, jnp.float32) * width * gain
    return jnp.minimum(jnp.maximum(values, -reach), reach).astype(held_as)


def setup_inputs(seed: int = 0, part: int = 0) -> dict:
    streams_of = jax.random.split(jax.random.key(seed), 6)
    part_splits = jax.random.split(jax.random.fold_in(streams_of[5], part), 6)
    return {
        "view_a": normal_values(part_splits[0], (HITS, D), 1.0, 6.0, ((0, 16),)),
        "view_b": normal_values(part_splits[1], (HITS, D), 1.0, 6.0, ((0, 16),)),
        "prototypes": normal_values(streams_of[2], (K, D), 1.0, 6.0, ((0, 4),)),
        "tile_mask": draw_tile_mask(jax.random.fold_in(streams_of[5], 71), part),
        "tile_region": draw_tile_region(jax.random.fold_in(jax.random.fold_in(streams_of[5], part), 71), part),
    }


SOFTMAX_TEMPER = 0.1
EPSILON = 0.05

def unit_rows(matrix):
    values = matrix.astype(jnp.float32)
    return (values * lax.rsqrt(lax.optimization_barrier(jnp.sum(values * values, axis=1, keepdims=True)) + 1e-06)).astype(jnp.bfloat16)

def reference(view_a, view_b, prototypes, tile_mask, tile_region):
    unit_a = unit_rows(view_a)
    unit_b = unit_rows(view_b)
    unit_protos = unit_rows(prototypes)
    block_cols = min(K, 1024)
    block_count = K // block_cols
    region_rows = jnp.repeat(tile_region, HIT_DEV)
    row_tiles = tile_mask[region_rows]
    block_ids = jnp.arange(block_count, dtype=jnp.int32)

    def block_pieces(block_index):
        col_block = lax.dynamic_slice_in_dim(unit_protos, (block_index * block_cols).astype(jnp.int32), block_cols, 0)
        flags = lax.dynamic_slice_in_dim(row_tiles, (block_index * (block_cols // TILE)).astype(jnp.int32), block_cols // TILE, 1)
        return (col_block, jnp.repeat(flags > 0, TILE, axis=1))

    def codes_block(block_index):
        col_block, live_block_mask = block_pieces(block_index)
        prototype_scores = jnp.dot(unit_a, col_block.T, preferred_element_type=jnp.float32)
        code_exp = jnp.where(live_block_mask, jnp.exp((prototype_scores - 1.0) / EPSILON), 0.0).astype(jnp.bfloat16)
        return lax.optimization_barrier(code_exp).astype(jnp.float32)

    def balancing_sweep(row_inverses):

        def pass_turn(running, block_index):
            code_exp = codes_block(block_index)
            column_inverses = 1.0 / lax.optimization_barrier(jnp.sum(code_exp * row_inverses[:, None], axis=0))
            return (running + lax.optimization_barrier(jnp.sum(code_exp * column_inverses[None, :], axis=1)), column_inverses)
        row_totals, column_inverses = lax.scan(pass_turn, jnp.zeros((HITS,), jnp.float32), block_ids)
        return (1.0 / row_totals, column_inverses.reshape(-1))

    def norm_turn(running, block_index):
        col_block, live_block_mask = block_pieces(block_index)
        prototype_scores = jnp.dot(unit_b, col_block.T, preferred_element_type=jnp.float32)
        prototype_weights = jnp.where(live_block_mask, jnp.exp((prototype_scores - 1.0) / SOFTMAX_TEMPER), 0.0)
        return (running + lax.optimization_barrier(jnp.sum(prototype_weights, axis=1)), None)
    second_view_norm, unused = lax.scan(norm_turn, jnp.zeros((HITS,), jnp.float32), block_ids)
    row_inverses = jnp.ones((HITS,), jnp.float32)
    column_inverses = jnp.ones((K,), jnp.float32)
    for sweep_index in range(ITERS):
        row_inverses, column_inverses = balancing_sweep(row_inverses)

    def grad_turn(running, block_index):
        col_block, live_block_mask = block_pieces(block_index)
        code_exp = codes_block(block_index)
        prototype_scores = jnp.dot(unit_b, col_block.T, preferred_element_type=jnp.float32)
        predicted_logits = jnp.where(live_block_mask, jnp.exp((prototype_scores - 1.0) / SOFTMAX_TEMPER), 0.0) / second_view_norm[:, None]
        recip_block = lax.dynamic_slice_in_dim(column_inverses, (block_index * block_cols).astype(jnp.int32), block_cols, 0)
        code_entries = row_inverses[:, None] * code_exp * recip_block[None, :]
        score_gradient = ((predicted_logits - code_entries) / SOFTMAX_TEMPER).astype(jnp.bfloat16)
        hit_part = jnp.dot(score_gradient, col_block, preferred_element_type=jnp.float32)
        proto_part = jnp.dot(score_gradient.T, unit_b, preferred_element_type=jnp.float32)
        return (running + hit_part, proto_part)
    grad_view_b, proto_parts = lax.scan(grad_turn, jnp.zeros((HITS, D), jnp.float32), block_ids)
    return (grad_view_b, proto_parts.reshape(K, D))
```

```python
import functools
import math

import jax
import jax.numpy as jnp
from jax import lax
from jax.experimental import pallas as pl
from jax.experimental.pallas import tpu as pltpu
from jax.sharding import PartitionSpec as P

TILE = 128
ITERS = 3
SOFTMAX_TEMPER = 0.1
EPSILON = 0.05
LOG2E = math.log2(math.e)
CODE_GAIN = LOG2E / EPSILON
PRED_GAIN = LOG2E / SOFTMAX_TEMPER
OFF = -1e30
MESH = pl.DeviceIdType.MESH
F32 = jnp.float32
BF16 = jnp.bfloat16


def unit_rows(matrix):
    values = matrix.astype(F32)
    return (values * lax.rsqrt(jnp.sum(values * values, axis=1, keepdims=True) + 1e-06)).astype(
        BF16
    )


def down_rows(row):
    return jnp.broadcast_to(row, (TILE, TILE)).T


def across_lanes(block):
    return jnp.sum(block.T, axis=0, keepdims=True)


def fold(block):
    return jnp.sum(block.reshape(block.shape[0] // 8, 8, block.shape[1]), axis=0)


def kernel(
    n_blk,
    n_dp,
    hit_dev,
    cols,
    region_ref,
    mask_ref,
    view_a_ref,
    view_b_ref,
    protos_ref,
    gview_ref,
    gproto_ref,
    rows_a,
    rows_b,
    protos,
    code,
    pred,
    lanes,
    colacc,
    colinv,
    rowinv,
    norminv,
    plane_msg,
    line_msg,
    hits2,
    red,
    s_in,
    x_in,
    z_out,
    z_in,
    load_sem,
    agz_send,
    agz_recv,
    agx_send,
    agx_recv,
    ags_send,
    ags_recv,
    arp_send,
    arp_recv,
    arz_send,
    arz_recv,
    rss_send,
    rss_recv,
    rsx_send,
    rsx_recv,
    rsz_send,
    rsz_recv,
):
    z = lax.axis_index("blk")
    x = lax.axis_index("dp")
    c = lax.axis_index("sub")
    plane = 2 * n_dp
    q = x * 2 + c
    group_rows = plane * hit_dev
    pairs = n_blk * n_dp
    tiles = cols // TILE
    first_tile = (z * plane + q) * tiles
    width = protos.shape[1]
    CC = min(1024, cols)
    ctiles = CC // TILE

    barrier = pltpu.get_barrier_semaphore()

    def plane_id(step):
        other = lax.rem(q + step, plane)
        return {"dp": lax.div(other, 2), "sub": lax.rem(other, 2)}

    def line_id(step):
        return {"blk": lax.rem(z + step, n_blk)}

    direct = n_blk * plane <= 16
    team = n_blk * plane if direct else plane
    me = z * plane + q if direct else q

    def team_id(step):
        if not direct:
            return plane_id(step)
        other = lax.rem(me + step, team)
        return {
            "blk": lax.div(other, plane),
            "dp": lax.rem(lax.div(other, 2), n_dp),
            "sub": lax.rem(other, 2),
        }

    for step in range(1, team):
        pl.semaphore_signal(barrier, inc=1, device_id=team_id(step), device_id_type=MESH)
    if not direct:
        for step in range(1, n_blk):
            pl.semaphore_signal(barrier, inc=1, device_id=line_id(step), device_id_type=MESH)

    load = pltpu.make_async_copy(protos_ref.at[pl.ds(q * cols, cols)], protos, load_sem)
    load.start()
    rows_a[z, x, c] = unit_rows(view_a_ref[...])
    rows_b[z, x, c] = unit_rows(view_b_ref[...])
    pl.semaphore_wait(barrier, team - 1 + (0 if direct else n_blk - 1))

    sends = []

    def send(src, dst, send_sem, recv_sem, device):
        copy = pltpu.make_async_remote_copy(
            src_ref=src,
            dst_ref=dst,
            send_sem=send_sem,
            recv_sem=recv_sem,
            device_id=device,
            device_id_type=MESH,
        )
        copy.start()
        sends.append(copy)
        return copy

    def arrive(dst, send_sem, recv_sem, device):
        pltpu.make_async_remote_copy(
            src_ref=dst,
            dst_ref=dst,
            send_sem=send_sem,
            recv_sem=recv_sem,
            device_id=device,
            device_id_type=MESH,
        ).wait_recv()

    sub_id = {"sub": 1 - c}

    def source(k):
        return lax.rem(z - k + n_blk, n_blk)

    def near(dx):
        return lax.rem(x - dx + n_dp, n_dp)

    def to_sub(v, rows, k, dx):
        ref = rows.at[source(k), near(dx), c]
        send(ref, ref, ags_send.at[v, k, dx], ags_recv.at[v, k, dx], sub_id)

    def gather_a(v, rows, k):
        ref = rows.at[source(k), x, c]
        if k == 0:
            for step in range(1, n_blk):
                send(ref, ref, agz_send.at[v, step], agz_recv.at[v, step], line_id(step))
        else:
            arrive(ref, agz_send.at[v, k], agz_recv.at[v, k], line_id(k))
        for dx in range(1, n_dp):
            send(
                ref,
                ref,
                agx_send.at[v, k, dx],
                agx_recv.at[v, k, dx],
                {"dp": lax.rem(x + dx, n_dp)},
            )
        to_sub(v, rows, k, 0)

    def gather_b(v, rows, k):
        for dx in range(1, n_dp):
            ref = rows.at[source(k), near(dx), c]
            arrive(
                ref,
                agx_send.at[v, k, dx],
                agx_recv.at[v, k, dx],
                {"dp": lax.rem(x + dx, n_dp)},
            )
            to_sub(v, rows, k, dx)

    def gather_c(v, rows, k):
        for dx in range(n_dp):
            ref = rows.at[source(k), near(dx), 1 - c]
            arrive(ref, ags_send.at[v, k, dx], ags_recv.at[v, k, dx], sub_id)

    def bias(pair, core, tile, gain):
        region = region_ref[pair * 2 + core]
        return jnp.where(mask_ref[region, first_tile + tile] > 0, -gain, OFF).astype(F32)

    def score(rows, zi, xs, count, col):
        left = rows[zi, pl.ds(xs, count)].reshape(count * 2 * hit_dev, width)
        right = protos[pl.ds(col, CC), :]
        return lax.dot_general(
            left, right, (((1,), (1,)), ((), ())), preferred_element_type=F32
        )

    PX = min(2, n_dp)

    def code_group(k):
        zi = source(k)

        def step(t, carry):
            xs = (t % (n_dp // PX)) * PX
            ci = t // (n_dp // PX)
            col = pl.multiple_of(ci * CC, CC)
            s = score(rows_a, zi, xs, PX, col)
            for j in range(ctiles):
                total = None
                lane = pl.ds(pl.multiple_of(col + j * TILE, TILE), TILE)
                for i in range(PX):
                    for core in range(2):
                        lo = (i * 2 + core) * hit_dev
                        piece = s[lo : lo + hit_dev, j * TILE : (j + 1) * TILE]
                        b = bias(zi * n_dp + xs + i, core, ci * ctiles + j, CODE_GAIN)
                        e = jnp.exp2(piece * CODE_GAIN + b).astype(BF16)
                        row = pl.multiple_of(zi * group_rows + xs * 2 * hit_dev + lo, hit_dev)
                        code[pl.ds(row, hit_dev), lane] = e
                        part = fold(e.astype(F32))
                        total = part if total is None else total + part
                colacc[:, lane] = colacc[:, lane] + total
            return carry

        lax.fori_loop(0, (n_dp // PX) * (cols // CC), step, 0)

    def pred_group(zi):
        def block(t, carry):
            xs = t * PX
            lanes[...] = jnp.zeros_like(lanes)

            def step(ci, inner):
                col = pl.multiple_of(ci * CC, CC)
                s = score(rows_b, zi, xs, PX, col)
                for i in range(PX):
                    for core in range(2):
                        lo = (i * 2 + core) * hit_dev
                        total = None
                        for j in range(ctiles):
                            piece = s[lo : lo + hit_dev, j * TILE : (j + 1) * TILE]
                            b = bias(zi * n_dp + xs + i, core, ci * ctiles + j, PRED_GAIN)
                            e = jnp.exp2(piece * PRED_GAIN + b)
                            row = pl.multiple_of(
                                zi * group_rows + xs * 2 * hit_dev + lo, hit_dev
                            )
                            lane = pl.ds(pl.multiple_of(col + j * TILE, TILE), TILE)
                            pred[pl.ds(row, hit_dev), lane] = e
                            total = e if total is None else total + e
                        lanes[lo : lo + hit_dev, :] = lanes[lo : lo + hit_dev, :] + total
                return inner

            lax.fori_loop(0, cols // CC, step, 0)
            for i in range(PX):
                norminv[pl.ds(zi * n_dp + xs + i, 1), :] = across_lanes(
                    lanes[i * TILE : (i + 1) * TILE, :]
                )
            return carry

        lax.fori_loop(0, n_dp // PX, block, 0)

    def close_columns():
        total = jnp.sum(colacc[...], axis=0, keepdims=True)
        colinv[...] = jnp.broadcast_to(1.0 / total, colinv.shape)

    def column_pass():
        colacc[...] = jnp.zeros_like(colacc)

        def step(p, carry):
            scale = down_rows(rowinv[pl.ds(p, 1), :])
            row = pl.ds(pl.multiple_of(p * TILE, TILE), TILE)
            for j in range(tiles):
                lane = slice(j * TILE, (j + 1) * TILE)
                colacc[:, lane] = colacc[:, lane] + fold(code[row, lane].astype(F32) * scale)
            return carry

        lax.fori_loop(0, pairs, step, 0)
        close_columns()

    def row_pass(sweep):
        def step(p, carry):
            row = pl.ds(pl.multiple_of(p * TILE, TILE), TILE)
            total = None
            for j in range(tiles):
                lane = slice(j * TILE, (j + 1) * TILE)
                part = code[row, lane].astype(F32) * colinv[0:1, lane]
                total = part if total is None else total + part
            plane_msg[sweep, me, pl.ds(p, 1), :] = across_lanes(total)
            return carry

        lax.fori_loop(0, pairs, step, 0)

    def reduce_start(sweep):
        size = 2 * pairs if sweep == ITERS - 1 else pairs
        mine = plane_msg.at[sweep, me, pl.ds(0, size)]
        for step in range(1, team):
            send(mine, mine, arp_send.at[sweep, step], arp_recv.at[sweep, step], team_id(step))

    def close_rows(sweep, total):
        rowinv[...] = 1.0 / total[0:pairs]
        if sweep == ITERS - 1:
            norminv[...] = (1.0 / SOFTMAX_TEMPER) / total[pairs : 2 * pairs]

    def reduce_middle(sweep):
        size = 2 * pairs if sweep == ITERS - 1 else pairs
        for step in range(1, team):
            other = plane_msg.at[sweep, lax.rem(me - step + team, team), pl.ds(0, size)]
            arrive(other, arp_send.at[sweep, step], arp_recv.at[sweep, step], team_id(step))
        total = plane_msg[sweep, 0, 0:size, :]
        for other in range(1, team):
            total = total + plane_msg[sweep, other, 0:size, :]
        if direct:
            close_rows(sweep, total)
            return
        line_msg[sweep, z, 0:size, :] = total
        mine = line_msg.at[sweep, z, pl.ds(0, size)]
        for step in range(1, n_blk):
            send(mine, mine, arz_send.at[sweep, step], arz_recv.at[sweep, step], line_id(step))

    def reduce_end(sweep):
        if direct:
            return
        size = 2 * pairs if sweep == ITERS - 1 else pairs
        for step in range(1, n_blk):
            other = line_msg.at[sweep, source(step), pl.ds(0, size)]
            arrive(other, arz_send.at[sweep, step], arz_recv.at[sweep, step], line_id(step))
        total = line_msg[sweep, 0, 0:size, :]
        for other in range(1, n_blk):
            total = total + line_msg[sweep, other, 0:size, :]
        close_rows(sweep, total)

    gather_a(0, rows_a, 0)
    load.wait()
    NC = min(256, cols)

    def normalize(t, carry):
        at = pl.ds(pl.multiple_of(t * NC, NC), NC)
        protos[at, :] = unit_rows(protos[at, :])
        return carry

    lax.fori_loop(0, cols // NC, normalize, 0)
    colacc[...] = jnp.zeros_like(colacc)
    gather_b(0, rows_a, 0)
    for k in range(n_blk):
        if k + 1 < n_blk:
            gather_a(0, rows_a, k + 1)
        if k == n_blk - 1:
            gather_a(1, rows_b, 0)
        gather_c(0, rows_a, k)
        code_group(k)
        if k + 1 < n_blk:
            gather_b(0, rows_a, k + 1)
    close_columns()
    for k in range(1, n_blk):
        gather_a(1, rows_b, k)
        gather_b(1, rows_b, k - 1)
    row_pass(0)
    reduce_start(0)
    gather_b(1, rows_b, n_blk - 1)
    for k in range(n_blk):
        gather_c(1, rows_b, k)

    share = [n_blk * i // 4 for i in range(5)]
    if direct:
        share = [0, n_blk // 2, n_blk // 2, n_blk, n_blk]
    part = 0
    for sweep in range(ITERS):
        if sweep > 0:
            column_pass()
            row_pass(sweep)
            if sweep == ITERS - 1:
                plane_msg[sweep, me, pairs : 2 * pairs, :] = norminv[...]
            reduce_start(sweep)
        if sweep < 2:
            for zi in range(share[part], share[part + 1]):
                pred_group(zi)
            part += 1
        reduce_middle(sweep)
        if sweep < 2:
            for zi in range(share[part], share[part + 1]):
                pred_group(zi)
            part += 1
        reduce_end(sweep)

    def grad_group(zi, slot):
        def rows_step(t, carry):
            p = zi * n_dp + t
            row = pl.ds(pl.multiple_of(p * TILE, TILE), TILE)
            scale = down_rows(rowinv[pl.ds(p, 1), :] * (1.0 / SOFTMAX_TEMPER))
            weight = down_rows(norminv[pl.ds(p, 1), :])
            for j in range(tiles):
                lane = slice(j * TILE, (j + 1) * TILE)
                codes = (code[row, lane].astype(F32) * scale) * colinv[0:1, lane]
                code[row, lane] = (pred[row, lane] * weight - codes).astype(BF16)
            return carry

        lax.fori_loop(0, n_dp, rows_step, 0)

        def dot_step(t, carry):
            xs = t * PX
            size = PX * 2 * hit_dev
            row = pl.multiple_of(zi * group_rows + xs * 2 * hit_dev, size)
            part = jnp.dot(code[pl.ds(row, size), :], protos[...], preferred_element_type=F32)
            for i in range(PX):
                for core in range(2):
                    lo = (i * 2 + core) * hit_dev
                    hits2[slot, core, xs + i] = part[lo : lo + hit_dev, :]
            return carry

        lax.fori_loop(0, n_dp // PX, dot_step, 0)

    SLOTS = hits2.shape[0]
    order = list(range(1, n_blk)) + [0]
    sub_sends = {}
    dp_sends = {}

    def drain(copies):
        for old in copies:
            old.wait_send()
            sends[:] = [copy for copy in sends if copy is not old]

    def scatter_start(i):
        k = order[i]
        slot = i % SLOTS
        if i >= SLOTS:
            drain([sub_sends[i - SLOTS]])
        grad_group(lax.rem(z + k, n_blk), slot)
        sub_sends[i] = send(
            hits2.at[slot, 1 - c], s_in.at[k], rss_send.at[k], rss_recv.at[k], sub_id
        )

    def scatter_sub(i):
        k = order[i]
        slot = i % SLOTS
        arrive(s_in.at[k], rss_send.at[k], rss_recv.at[k], sub_id)
        if i >= SLOTS:
            drain(dp_sends[i - SLOTS])
        red[slot] = hits2[slot, c] + s_in[k]
        dp_sends[i] = []
        for dx in range(1, n_dp):
            other = lax.rem(x + dx, n_dp)
            dp_sends[i].append(
                send(
                    red.at[slot, other],
                    x_in.at[k, dx - 1],
                    rsx_send.at[k, dx],
                    rsx_recv.at[k, dx],
                    {"dp": other},
                )
            )

    def scatter_dp(i):
        k = order[i]
        total = red[i % SLOTS, x]
        for dx in range(1, n_dp):
            other = lax.rem(x + dx, n_dp)
            arrive(x_in.at[k, dx - 1], rsx_send.at[k, dx], rsx_recv.at[k, dx], {"dp": other})
            total = total + x_in[k, dx - 1]
        z_out[k] = total
        if k > 0:
            send(z_out.at[k], z_in.at[k], rsz_send.at[k], rsz_recv.at[k], line_id(k))

    PC = min(512, cols)

    def proto_cols(t, carry):
        lane = pl.ds(pl.multiple_of(t * PC, PC), PC)
        total = None
        for zi in range(n_blk):
            left = code[zi * group_rows : (zi + 1) * group_rows, lane]
            right = rows_b[zi].reshape(group_rows, width)
            part = lax.dot_general(
                left, right, (((0,), (0,)), ((), ())), preferred_element_type=F32
            )
            total = part if total is None else total + part
        gproto_ref[lane, :] = total
        return carry

    for i in range(n_blk):
        scatter_start(i)
        if i >= 1:
            scatter_sub(i - 1)
        if i >= 2:
            scatter_dp(i - 2)
    chunks = cols // PC
    cut = [chunks * i // 4 for i in range(5)]
    lax.fori_loop(cut[0], cut[1], proto_cols, 0)
    scatter_sub(n_blk - 1)
    if n_blk >= 2:
        scatter_dp(n_blk - 2)
    lax.fori_loop(cut[1], cut[2], proto_cols, 0)
    scatter_dp(n_blk - 1)
    lax.fori_loop(cut[2], cut[4], proto_cols, 0)
    total = z_out[0]
    for k in range(1, n_blk):
        arrive(z_in.at[k], rsz_send.at[k], rsz_recv.at[k], line_id(k))
        total = total + z_in[k]
    gview_ref[...] = total
    for copy in sends:
        copy.wait_send()


def kernel_direct(
    n_blk,
    n_dp,
    hit_dev,
    cols,
    region_hbm,
    mask_hbm,
    view_a_hbm,
    view_b_hbm,
    protos_ref,
    gview_ref,
    gproto_ref,
    region_ref,
    mask_ref,
    view_a_ref,
    view_b_ref,
    rows_a,
    rows_b,
    protos,
    code,
    pred,
    lanes,
    colacc,
    colinv,
    rowinv,
    norminv,
    plane_msg,
    hits2,
    red,
    s_in,
    x_in,
    z_out,
    z_in,
    load_sem,
    agz_send,
    agz_recv,
    agx_send,
    agx_recv,
    ags_send,
    ags_recv,
    arp_send,
    arp_recv,
    rss_send,
    rss_recv,
    rsx_send,
    rsx_recv,
    rsz_send,
    rsz_recv,
):
    z = lax.axis_index("blk")
    x = lax.axis_index("dp")
    c = lax.axis_index("sub")
    plane = 2 * n_dp
    q = x * 2 + c
    group_rows = plane * hit_dev
    pairs = n_blk * n_dp
    tiles = cols // TILE
    first_tile = (z * plane + q) * tiles
    width = protos.shape[1]
    CC = min(1024, cols)
    ctiles = CC // TILE

    barrier = pltpu.get_barrier_semaphore()

    def visit(s):
        room = jnp.minimum(z, n_blk - 1 - z)
        half = (s + 1) // 2
        near = z + half if s % 2 else z - half
        far = jnp.where(2 * z < n_blk - 1, z + (s - room), z - (s - room))
        return jnp.where(s <= 2 * room, near, far)

    near_z = [z] + [visit(s) for s in range(1, n_blk)]
    team = n_blk * plane
    me = z * plane + q

    def team_at(zi, dx, dc):
        xi = lax.rem(x + dx, n_dp)
        ci = 1 - c if dc else c
        return zi * plane + xi * 2 + ci, {"blk": zi, "dp": xi, "sub": ci}

    peers = []
    for s in reversed(range(n_blk)):
        for dx in reversed(range(n_dp)):
            for dc in range(2):
                if s or dx or dc:
                    peers.append(team_at(near_z[s], dx, dc))

    loads = []
    for index, (src, dst) in enumerate(
        (
            (view_a_hbm, view_a_ref),
            (protos_ref.at[pl.ds(q * cols, cols)], protos),
            (view_b_hbm, view_b_ref),
            (region_hbm, region_ref),
            (mask_hbm, mask_ref),
        )
    ):
        load = pltpu.make_async_copy(src, dst, load_sem.at[index])
        load.start()
        loads.append(load)
    for _, device in peers:
        pl.semaphore_signal(barrier, inc=1, device_id=device, device_id_type=MESH)
    loads[0].wait()
    rows_a[z, x, c] = unit_rows(view_a_ref[...])
    loads[2].wait()
    rows_b[z, x, c] = unit_rows(view_b_ref[...])
    pl.semaphore_wait(barrier, team - 1)

    sends = []

    def send(src, dst, send_sem, recv_sem, device):
        copy = pltpu.make_async_remote_copy(
            src_ref=src,
            dst_ref=dst,
            send_sem=send_sem,
            recv_sem=recv_sem,
            device_id=device,
            device_id_type=MESH,
        )
        copy.start()
        sends.append(copy)
        return copy

    def arrive(dst, send_sem, recv_sem, device):
        pltpu.make_async_remote_copy(
            src_ref=dst,
            dst_ref=dst,
            send_sem=send_sem,
            recv_sem=recv_sem,
            device_id=device,
            device_id_type=MESH,
        ).wait_recv()

    sub_id = {"sub": 1 - c}

    def to_sub(v, rows, zi, xi):
        ref = rows.at[zi, xi, c]
        send(ref, ref, ags_send.at[v, zi, xi], ags_recv.at[v, zi, xi], sub_id)

    def to_x(v, rows, zi):
        ref = rows.at[zi, x, c]
        for dx in range(1, n_dp):
            xi = lax.rem(x + dx, n_dp)
            send(ref, ref, agx_send.at[v, zi, xi], agx_recv.at[v, zi, x], {"dp": xi})

    def gather_own(v, rows):
        ref = rows.at[z, x, c]
        for s in reversed(range(1, n_blk)):
            zi = near_z[s]
            send(ref, ref, agz_send.at[v, zi], agz_recv.at[v, z], {"blk": zi})
        to_x(v, rows, z)
        to_sub(v, rows, z, x)

    def gather_z(v, rows, s):
        zi = near_z[s]
        arrive(rows.at[zi, x, c], agz_send.at[v, zi], agz_recv.at[v, zi], {"blk": zi})
        to_x(v, rows, zi)
        to_sub(v, rows, zi, x)

    def gather_x(v, rows, s):
        zi = near_z[s]
        for dx in range(1, n_dp):
            xi = lax.rem(x + n_dp - dx, n_dp)
            arrive(
                rows.at[zi, xi, c], agx_send.at[v, zi, xi], agx_recv.at[v, zi, xi], {"dp": xi}
            )
            to_sub(v, rows, zi, xi)

    def gather_sub(v, rows, s):
        zi = near_z[s]
        for dx in range(n_dp):
            xi = lax.rem(x + dx, n_dp)
            ref = rows.at[zi, xi, 1 - c]
            arrive(ref, ags_send.at[v, zi, xi], ags_recv.at[v, zi, xi], sub_id)

    def bias(pair, core, tile, gain):
        region = region_ref[pair * 2 + core]
        return jnp.where(mask_ref[region, first_tile + tile] > 0, -gain, OFF).astype(F32)

    def score(rows, zi, xs, count, col):
        left = rows[zi, pl.ds(xs, count)].reshape(count * 2 * hit_dev, width)
        right = protos[pl.ds(col, CC), :]
        return lax.dot_general(
            left, right, (((1,), (1,)), ((), ())), preferred_element_type=F32
        )

    PX = min(2, n_dp)

    def code_group(zi):

        def step(t, carry):
            xs = (t % (n_dp // PX)) * PX
            ci = t // (n_dp // PX)
            col = pl.multiple_of(ci * CC, CC)
            s = score(rows_a, zi, xs, PX, col)
            for j in range(ctiles):
                total = None
                lane = pl.ds(pl.multiple_of(col + j * TILE, TILE), TILE)
                for i in range(PX):
                    for core in range(2):
                        lo = (i * 2 + core) * hit_dev
                        piece = s[lo : lo + hit_dev, j * TILE : (j + 1) * TILE]
                        b = bias(zi * n_dp + xs + i, core, ci * ctiles + j, CODE_GAIN)
                        e = jnp.exp2(piece * CODE_GAIN + b).astype(BF16)
                        row = pl.multiple_of(zi * group_rows + xs * 2 * hit_dev + lo, hit_dev)
                        code[pl.ds(row, hit_dev), lane] = e
                        part = fold(e.astype(F32))
                        total = part if total is None else total + part
                colacc[:, lane] = colacc[:, lane] + total
            return carry

        lax.fori_loop(0, (n_dp // PX) * (cols // CC), step, 0)

    def pred_group(zi):
        def block(t, carry):
            xs = t * PX
            lanes[...] = jnp.zeros_like(lanes)

            def step(ci, inner):
                col = pl.multiple_of(ci * CC, CC)
                s = score(rows_b, zi, xs, PX, col)
                for i in range(PX):
                    for core in range(2):
                        lo = (i * 2 + core) * hit_dev
                        total = None
                        for j in range(ctiles):
                            piece = s[lo : lo + hit_dev, j * TILE : (j + 1) * TILE]
                            b = bias(zi * n_dp + xs + i, core, ci * ctiles + j, PRED_GAIN)
                            e = jnp.exp2(piece * PRED_GAIN + b)
                            row = pl.multiple_of(
                                zi * group_rows + xs * 2 * hit_dev + lo, hit_dev
                            )
                            lane = pl.ds(pl.multiple_of(col + j * TILE, TILE), TILE)
                            pred[pl.ds(row, hit_dev), lane] = e
                            total = e if total is None else total + e
                        lanes[lo : lo + hit_dev, :] = lanes[lo : lo + hit_dev, :] + total
                return inner

            lax.fori_loop(0, cols // CC, step, 0)
            for i in range(PX):
                norminv[pl.ds(zi * n_dp + xs + i, 1), :] = across_lanes(
                    lanes[i * TILE : (i + 1) * TILE, :]
                )
            return carry

        lax.fori_loop(0, n_dp // PX, block, 0)

    def close_columns():
        total = jnp.sum(colacc[...], axis=0, keepdims=True)
        colinv[...] = jnp.broadcast_to(1.0 / total, colinv.shape)

    def column_pass():
        colacc[...] = jnp.zeros_like(colacc)

        def step(p, carry):
            scale = down_rows(rowinv[pl.ds(p, 1), :])
            row = pl.ds(pl.multiple_of(p * TILE, TILE), TILE)
            for j in range(tiles):
                lane = slice(j * TILE, (j + 1) * TILE)
                colacc[:, lane] = colacc[:, lane] + fold(code[row, lane].astype(F32) * scale)
            return carry

        lax.fori_loop(0, pairs, step, 0)
        close_columns()

    def row_pass(sweep):
        def step(p, carry):
            row = pl.ds(pl.multiple_of(p * TILE, TILE), TILE)
            total = None
            for j in range(tiles):
                lane = slice(j * TILE, (j + 1) * TILE)
                part = code[row, lane].astype(F32) * colinv[0:1, lane]
                total = part if total is None else total + part
            plane_msg[sweep, me, pl.ds(p, 1), :] = across_lanes(total)
            return carry

        lax.fori_loop(0, pairs, step, 0)

    def reduce_start(sweep):
        size = 2 * pairs if sweep == ITERS - 1 else pairs
        mine = plane_msg.at[sweep, me, pl.ds(0, size)]
        for other, device in peers:
            send(mine, mine, arp_send.at[sweep, other], arp_recv.at[sweep, me], device)

    def reduce_end(sweep):
        size = 2 * pairs if sweep == ITERS - 1 else pairs
        for other, device in reversed(peers):
            ref = plane_msg.at[sweep, other, pl.ds(0, size)]
            arrive(ref, arp_send.at[sweep, other], arp_recv.at[sweep, other], device)
        total = plane_msg[sweep, 0, 0:size, :]
        for other in range(1, team):
            total = total + plane_msg[sweep, other, 0:size, :]
        rowinv[...] = 1.0 / total[0:pairs]
        if sweep == ITERS - 1:
            norminv[...] = (1.0 / SOFTMAX_TEMPER) / total[pairs : 2 * pairs]

    gather_own(0, rows_a)
    gather_own(1, rows_b)
    loads[1].wait()
    NC = min(256, cols)

    def normalize(t, carry):
        at = pl.ds(pl.multiple_of(t * NC, NC), NC)
        protos[at, :] = unit_rows(protos[at, :])
        return carry

    lax.fori_loop(0, cols // NC, normalize, 0)
    colacc[...] = jnp.zeros_like(colacc)
    loads[3].wait()
    loads[4].wait()
    for s in range(1, n_blk):
        gather_z(0, rows_a, s)
        if s == 1:
            gather_x(0, rows_a, 0)
    gather_sub(0, rows_a, 0)
    code_group(near_z[0])
    for s in range(1, n_blk):
        gather_x(0, rows_a, s)
        if s >= 2:
            gather_sub(0, rows_a, s - 1)
            code_group(near_z[s - 1])
    for s in range(1, n_blk):
        gather_z(1, rows_b, s)
    gather_x(1, rows_b, 0)
    if n_blk > 1:
        gather_sub(0, rows_a, n_blk - 1)
        code_group(near_z[n_blk - 1])
    close_columns()
    row_pass(0)
    reduce_start(0)
    for s in range(1, n_blk):
        gather_x(1, rows_b, s)
    for s in range(n_blk):
        gather_sub(1, rows_b, s)

    share = [0, n_blk // 2, n_blk]
    for sweep in range(ITERS):
        if sweep > 0:
            column_pass()
            row_pass(sweep)
            if sweep == ITERS - 1:
                plane_msg[sweep, me, pairs : 2 * pairs, :] = norminv[...]
            reduce_start(sweep)
        if sweep < 2:
            for s in range(share[sweep], share[sweep + 1]):
                pred_group(near_z[s])
        reduce_end(sweep)

    def grad_group(zi, slot):
        def rows_step(t, carry):
            p = zi * n_dp + t
            row = pl.ds(pl.multiple_of(p * TILE, TILE), TILE)
            scale = down_rows(rowinv[pl.ds(p, 1), :] * (1.0 / SOFTMAX_TEMPER))
            weight = down_rows(norminv[pl.ds(p, 1), :])
            for j in range(tiles):
                lane = slice(j * TILE, (j + 1) * TILE)
                codes = (code[row, lane].astype(F32) * scale) * colinv[0:1, lane]
                code[row, lane] = (pred[row, lane] * weight - codes).astype(BF16)
            return carry

        lax.fori_loop(0, n_dp, rows_step, 0)

        def dot_step(t, carry):
            xs = t * PX
            size = PX * 2 * hit_dev
            row = pl.multiple_of(zi * group_rows + xs * 2 * hit_dev, size)
            part = jnp.dot(code[pl.ds(row, size), :], protos[...], preferred_element_type=F32)
            for i in range(PX):
                for core in range(2):
                    lo = (i * 2 + core) * hit_dev
                    hits2[slot, core, xs + i] = part[lo : lo + hit_dev, :]
            return carry

        lax.fori_loop(0, n_dp // PX, dot_step, 0)

    SLOTS = hits2.shape[0]
    order = list(reversed(range(n_blk)))
    sub_sends = {}
    dp_sends = {}

    def drain(copies):
        for old in copies:
            old.wait_send()
            sends[:] = [copy for copy in sends if copy is not old]

    def scatter_start(i):
        k = order[i]
        slot = i % SLOTS
        if i >= SLOTS:
            drain([sub_sends[i - SLOTS]])
        grad_group(near_z[k], slot)
        sub_sends[i] = send(
            hits2.at[slot, 1 - c], s_in.at[k], rss_send.at[k], rss_recv.at[k], sub_id
        )

    def scatter_sub(i):
        k = order[i]
        slot = i % SLOTS
        arrive(s_in.at[k], rss_send.at[k], rss_recv.at[k], sub_id)
        if i >= SLOTS:
            drain(dp_sends[i - SLOTS])
        red[slot] = hits2[slot, c] + s_in[k]
        dp_sends[i] = []
        for dx in range(1, n_dp):
            other = lax.rem(x + dx, n_dp)
            dp_sends[i].append(
                send(
                    red.at[slot, other],
                    x_in.at[k, dx - 1],
                    rsx_send.at[k, dx],
                    rsx_recv.at[k, dx],
                    {"dp": other},
                )
            )

    def scatter_dp(i):
        k = order[i]
        total = red[i % SLOTS, x]
        for dx in range(1, n_dp):
            other = lax.rem(x + dx, n_dp)
            arrive(x_in.at[k, dx - 1], rsx_send.at[k, dx], rsx_recv.at[k, dx], {"dp": other})
            total = total + x_in[k, dx - 1]
        z_out[k] = total
        if k > 0:
            zi = near_z[k]
            send(z_out.at[k], z_in.at[z], rsz_send.at[zi], rsz_recv.at[z], {"blk": zi})

    PC = min(512, cols)

    def proto_cols(t, carry):
        lane = pl.ds(pl.multiple_of(t * PC, PC), PC)
        total = None
        for zi in range(n_blk):
            left = code[zi * group_rows : (zi + 1) * group_rows, lane]
            right = rows_b[zi].reshape(group_rows, width)
            part = lax.dot_general(
                left, right, (((0,), (0,)), ((), ())), preferred_element_type=F32
            )
            total = part if total is None else total + part
        gproto_ref[lane, :] = total
        return carry

    for i in range(n_blk):
        scatter_start(i)
        if i >= 1:
            scatter_sub(i - 1)
        if i >= 2:
            scatter_dp(i - 2)
    chunks = cols // PC
    cut = [chunks * i // 4 for i in range(5)]
    lax.fori_loop(cut[0], cut[1], proto_cols, 0)
    scatter_sub(n_blk - 1)
    if n_blk >= 2:
        scatter_dp(n_blk - 2)
    lax.fori_loop(cut[1], cut[2], proto_cols, 0)
    scatter_dp(n_blk - 1)
    lax.fori_loop(cut[2], cut[4], proto_cols, 0)
    total = z_out[0]
    for k in range(1, n_blk):
        zi = near_z[k]
        arrive(z_in.at[zi], rsz_send.at[zi], rsz_recv.at[zi], {"blk": zi})
        total = total + z_in[zi]
    gview_ref[...] = total
    for copy in sends:
        copy.wait_send()


def body_direct(view_a, view_b, prototypes, tile_mask, tile_region):
    n_blk = lax.axis_size("blk")
    n_dp = lax.axis_size("dp")
    hit_dev, width = view_a.shape
    plane = 2 * n_dp
    cols = prototypes.shape[0] // plane
    pairs = n_blk * n_dp
    hits = pairs * 2 * hit_dev
    team = n_blk * plane
    slots = n_blk if n_blk <= 4 else 2
    dma = pltpu.SemaphoreType.DMA
    vmem = pl.BlockSpec(memory_space=pltpu.VMEM)
    anyw = pl.BlockSpec(memory_space=pl.ANY)
    return pl.pallas_call(
        functools.partial(kernel_direct, n_blk, n_dp, hit_dev, cols),
        out_shape=(
            jax.ShapeDtypeStruct((hit_dev, width), F32),
            jax.ShapeDtypeStruct((cols, width), F32),
        ),
        in_specs=[anyw] * 5,
        out_specs=(vmem, vmem),
        scratch_shapes=[
            pltpu.SMEM(tile_region.shape, jnp.int32),
            pltpu.SMEM(tile_mask.shape, jnp.int32),
            pltpu.VMEM((hit_dev, width), BF16),
            pltpu.VMEM((hit_dev, width), BF16),
            pltpu.VMEM((n_blk, n_dp, 2, hit_dev, width), BF16),
            pltpu.VMEM((n_blk, n_dp, 2, hit_dev, width), BF16),
            pltpu.VMEM((cols, width), BF16),
            pltpu.VMEM((hits, cols), BF16),
            pltpu.VMEM((hits, cols), F32),
            pltpu.VMEM((min(2, n_dp) * 2 * hit_dev, TILE), F32),
            pltpu.VMEM((8, cols), F32),
            pltpu.VMEM((8, cols), F32),
            pltpu.VMEM((pairs, TILE), F32),
            pltpu.VMEM((pairs, TILE), F32),
            pltpu.VMEM((ITERS, team, 2 * pairs, TILE), F32),
            pltpu.VMEM((slots, 2, n_dp, hit_dev, width), F32),
            pltpu.VMEM((slots, n_dp, hit_dev, width), F32),
            pltpu.VMEM((n_blk, n_dp, hit_dev, width), F32),
            pltpu.VMEM((n_blk, n_dp - 1, hit_dev, width), F32),
            pltpu.VMEM((n_blk, hit_dev, width), F32),
            pltpu.VMEM((n_blk, hit_dev, width), F32),
            dma((5,)),
            dma((2, n_blk)),
            dma((2, n_blk)),
            dma((2, n_blk, n_dp)),
            dma((2, n_blk, n_dp)),
            dma((2, n_blk, n_dp)),
            dma((2, n_blk, n_dp)),
            dma((ITERS, team)),
            dma((ITERS, team)),
            dma((n_blk,)),
            dma((n_blk,)),
            dma((n_blk, n_dp)),
            dma((n_blk, n_dp)),
            dma((n_blk,)),
            dma((n_blk,)),
        ],
        compiler_params=pltpu.CompilerParams(
            collective_id=0, has_side_effects=True, vmem_limit_bytes=50 << 20
        ),
    )(tile_region, tile_mask, view_a, view_b, prototypes)


def body(view_a, view_b, prototypes, tile_mask, tile_region):
    n_blk = lax.axis_size("blk")
    n_dp = lax.axis_size("dp")
    hit_dev, width = view_a.shape
    plane = 2 * n_dp
    cols = prototypes.shape[0] // plane
    pairs = n_blk * n_dp
    hits = pairs * 2 * hit_dev
    team = n_blk * plane if n_blk * plane <= 16 else plane
    slots = n_blk if n_blk <= 4 else 2
    dma = pltpu.SemaphoreType.DMA
    vmem = pl.BlockSpec(memory_space=pltpu.VMEM)
    smem = pl.BlockSpec(memory_space=pltpu.SMEM)
    return pl.pallas_call(
        functools.partial(kernel, n_blk, n_dp, hit_dev, cols),
        out_shape=(
            jax.ShapeDtypeStruct((hit_dev, width), F32),
            jax.ShapeDtypeStruct((cols, width), F32),
        ),
        in_specs=[smem, smem, vmem, vmem, pl.BlockSpec(memory_space=pl.ANY)],
        out_specs=(vmem, vmem),
        scratch_shapes=[
            pltpu.VMEM((n_blk, n_dp, 2, hit_dev, width), BF16),
            pltpu.VMEM((n_blk, n_dp, 2, hit_dev, width), BF16),
            pltpu.VMEM((cols, width), BF16),
            pltpu.VMEM((hits, cols), BF16),
            pltpu.VMEM((hits, cols), F32),
            pltpu.VMEM((min(2, n_dp) * 2 * hit_dev, TILE), F32),
            pltpu.VMEM((8, cols), F32),
            pltpu.VMEM((8, cols), F32),
            pltpu.VMEM((pairs, TILE), F32),
            pltpu.VMEM((pairs, TILE), F32),
            pltpu.VMEM((ITERS, team, 2 * pairs, TILE), F32),
            pltpu.VMEM((ITERS, n_blk, 2 * pairs, TILE), F32),
            pltpu.VMEM((slots, 2, n_dp, hit_dev, width), F32),
            pltpu.VMEM((slots, n_dp, hit_dev, width), F32),
            pltpu.VMEM((n_blk, n_dp, hit_dev, width), F32),
            pltpu.VMEM((n_blk, n_dp - 1, hit_dev, width), F32),
            pltpu.VMEM((n_blk, hit_dev, width), F32),
            pltpu.VMEM((n_blk, hit_dev, width), F32),
            dma,
            dma((2, n_blk)),
            dma((2, n_blk)),
            dma((2, n_blk, n_dp)),
            dma((2, n_blk, n_dp)),
            dma((2, n_blk, n_dp)),
            dma((2, n_blk, n_dp)),
            dma((ITERS, team)),
            dma((ITERS, team)),
            dma((ITERS, n_blk)),
            dma((ITERS, n_blk)),
            dma((n_blk,)),
            dma((n_blk,)),
            dma((n_blk, n_dp)),
            dma((n_blk, n_dp)),
            dma((n_blk,)),
            dma((n_blk,)),
        ],
        compiler_params=pltpu.CompilerParams(
            collective_id=0, has_side_effects=True, vmem_limit_bytes=(50 if team > plane else 62) << 20
        ),
    )(tile_region, tile_mask, view_a, view_b, prototypes)


def solution(mesh):
    small = mesh.shape["blk"] * mesh.shape["dp"] * mesh.shape["sub"] <= 16
    spread = P(("groups", "blk", "dp", "sub"), None)
    return jax.shard_map(
        body_direct if small else body,
        mesh=mesh,
        in_specs=(spread, spread, P("blk", None), P(), P("groups")),
        out_specs=(spread, spread),
        check_vma=False,
    )
```

```python
import functools
import math

import jax
import jax.numpy as jnp
from jax import lax
from jax.experimental import pallas as pl
from jax.experimental.pallas import tpu as pltpu
from jax.sharding import PartitionSpec as P

TILE = 128
ITERS = 3
SOFTMAX_TEMPER = 0.1
EPSILON = 0.05
LOG2E = math.log2(math.e)
CODE_GAIN = LOG2E / EPSILON
PRED_GAIN = LOG2E / SOFTMAX_TEMPER
OFF = -1e30
MESH = pl.DeviceIdType.MESH
F32 = jnp.float32
BF16 = jnp.bfloat16


def unit_rows(matrix):
    values = matrix.astype(F32)
    return (values * lax.rsqrt(jnp.sum(values * values, axis=1, keepdims=True) + 1e-06)).astype(
        BF16
    )


def down_rows(row):
    return jnp.broadcast_to(row, (TILE, TILE)).T


def across_lanes(block):
    return jnp.sum(block.T, axis=0, keepdims=True)


def fold(block):
    return jnp.sum(block.reshape(block.shape[0] // 8, 8, block.shape[1]), axis=0)


def kernel(
    n_blk,
    n_dp,
    hit_dev,
    cols,
    region_ref,
    mask_ref,
    view_a_ref,
    view_b_ref,
    protos_ref,
    gview_ref,
    gproto_ref,
    rows_a,
    rows_b,
    protos,
    code,
    pred,
    lanes,
    colacc,
    colinv,
    rowinv,
    norminv,
    plane_msg,
    line_msg,
    hits2,
    red,
    s_in,
    x_in,
    z_out,
    z_in,
    load_sem,
    agz_send,
    agz_recv,
    agx_send,
    agx_recv,
    ags_send,
    ags_recv,
    arp_send,
    arp_recv,
    arz_send,
    arz_recv,
    rss_send,
    rss_recv,
    rsx_send,
    rsx_recv,
    rsz_send,
    rsz_recv,
):
    z = lax.axis_index("blk")
    x = lax.axis_index("dp")
    c = lax.axis_index("sub")
    plane = 2 * n_dp
    q = x * 2 + c
    group_rows = plane * hit_dev
    pairs = n_blk * n_dp
    tiles = cols // TILE
    first_tile = (z * plane + q) * tiles
    width = protos.shape[1]
    CC = min(1024, cols)
    ctiles = CC // TILE

    barrier = pltpu.get_barrier_semaphore()

    def plane_id(step):
        other = lax.rem(q + step, plane)
        return {"dp": lax.div(other, 2), "sub": lax.rem(other, 2)}

    def line_id(step):
        return {"blk": lax.rem(z + step, n_blk)}

    direct = n_blk * plane <= 16
    team = n_blk * plane if direct else plane
    me = z * plane + q if direct else q

    def team_id(step):
        if not direct:
            return plane_id(step)
        other = lax.rem(me + step, team)
        return {
            "blk": lax.div(other, plane),
            "dp": lax.rem(lax.div(other, 2), n_dp),
            "sub": lax.rem(other, 2),
        }

    for step in range(1, team):
        pl.semaphore_signal(barrier, inc=1, device_id=team_id(step), device_id_type=MESH)
    if not direct:
        for step in range(1, n_blk):
            pl.semaphore_signal(barrier, inc=1, device_id=line_id(step), device_id_type=MESH)

    load = pltpu.make_async_copy(protos_ref.at[pl.ds(q * cols, cols)], protos, load_sem)
    load.start()
    rows_a[z, x, c] = unit_rows(view_a_ref[...])
    rows_b[z, x, c] = unit_rows(view_b_ref[...])
    pl.semaphore_wait(barrier, team - 1 + (0 if direct else n_blk - 1))

    sends = []

    def send(src, dst, send_sem, recv_sem, device):
        copy = pltpu.make_async_remote_copy(
            src_ref=src,
            dst_ref=dst,
            send_sem=send_sem,
            recv_sem=recv_sem,
            device_id=device,
            device_id_type=MESH,
        )
        copy.start()
        sends.append(copy)
        return copy

    def arrive(dst, send_sem, recv_sem, device):
        pltpu.make_async_remote_copy(
            src_ref=dst,
            dst_ref=dst,
            send_sem=send_sem,
            recv_sem=recv_sem,
            device_id=device,
            device_id_type=MESH,
        ).wait_recv()

    sub_id = {"sub": 1 - c}

    def source(k):
        return lax.rem(z - k + n_blk, n_blk)

    def near(dx):
        return lax.rem(x - dx + n_dp, n_dp)

    def to_sub(v, rows, k, dx):
        ref = rows.at[source(k), near(dx), c]
        send(ref, ref, ags_send.at[v, k, dx], ags_recv.at[v, k, dx], sub_id)

    def gather_a(v, rows, k):
        ref = rows.at[source(k), x, c]
        if k == 0:
            for step in range(1, n_blk):
                send(ref, ref, agz_send.at[v, step], agz_recv.at[v, step], line_id(step))
        else:
            arrive(ref, agz_send.at[v, k], agz_recv.at[v, k], line_id(k))
        for dx in range(1, n_dp):
            send(
                ref,
                ref,
                agx_send.at[v, k, dx],
                agx_recv.at[v, k, dx],
                {"dp": lax.rem(x + dx, n_dp)},
            )
        to_sub(v, rows, k, 0)

    def gather_b(v, rows, k):
        for dx in range(1, n_dp):
            ref = rows.at[source(k), near(dx), c]
            arrive(
                ref,
                agx_send.at[v, k, dx],
                agx_recv.at[v, k, dx],
                {"dp": lax.rem(x + dx, n_dp)},
            )
            to_sub(v, rows, k, dx)

    def gather_c(v, rows, k):
        for dx in range(n_dp):
            ref = rows.at[source(k), near(dx), 1 - c]
            arrive(ref, ags_send.at[v, k, dx], ags_recv.at[v, k, dx], sub_id)

    def bias(pair, core, tile, gain):
        region = region_ref[pair * 2 + core]
        return jnp.where(mask_ref[region, first_tile + tile] > 0, -gain, OFF).astype(F32)

    def score(rows, zi, xs, count, col):
        left = rows[zi, pl.ds(xs, count)].reshape(count * 2 * hit_dev, width)
        right = protos[pl.ds(col, CC), :]
        return lax.dot_general(
            left, right, (((1,), (1,)), ((), ())), preferred_element_type=F32
        )

    PX = min(2, n_dp)

    def code_group(k):
        zi = source(k)

        def step(t, carry):
            xs = (t % (n_dp // PX)) * PX
            ci = t // (n_dp // PX)
            col = pl.multiple_of(ci * CC, CC)
            s = score(rows_a, zi, xs, PX, col)
            for j in range(ctiles):
                total = None
                lane = pl.ds(pl.multiple_of(col + j * TILE, TILE), TILE)
                for i in range(PX):
                    for core in range(2):
                        lo = (i * 2 + core) * hit_dev
                        piece = s[lo : lo + hit_dev, j * TILE : (j + 1) * TILE]
                        b = bias(zi * n_dp + xs + i, core, ci * ctiles + j, CODE_GAIN)
                        e = jnp.exp2(piece * CODE_GAIN + b).astype(BF16)
                        row = pl.multiple_of(zi * group_rows + xs * 2 * hit_dev + lo, hit_dev)
                        code[pl.ds(row, hit_dev), lane] = e
                        part = fold(e.astype(F32))
                        total = part if total is None else total + part
                colacc[:, lane] = colacc[:, lane] + total
            return carry

        lax.fori_loop(0, (n_dp // PX) * (cols // CC), step, 0)

    def pred_group(zi):
        def block(t, carry):
            xs = t * PX
            lanes[...] = jnp.zeros_like(lanes)

            def step(ci, inner):
                col = pl.multiple_of(ci * CC, CC)
                s = score(rows_b, zi, xs, PX, col)
                for i in range(PX):
                    for core in range(2):
                        lo = (i * 2 + core) * hit_dev
                        total = None
                        for j in range(ctiles):
                            piece = s[lo : lo + hit_dev, j * TILE : (j + 1) * TILE]
                            b = bias(zi * n_dp + xs + i, core, ci * ctiles + j, PRED_GAIN)
                            e = jnp.exp2(piece * PRED_GAIN + b)
                            row = pl.multiple_of(
                                zi * group_rows + xs * 2 * hit_dev + lo, hit_dev
                            )
                            lane = pl.ds(pl.multiple_of(col + j * TILE, TILE), TILE)
                            pred[pl.ds(row, hit_dev), lane] = e
                            total = e if total is None else total + e
                        lanes[lo : lo + hit_dev, :] = lanes[lo : lo + hit_dev, :] + total
                return inner

            lax.fori_loop(0, cols // CC, step, 0)
            for i in range(PX):
                norminv[pl.ds(zi * n_dp + xs + i, 1), :] = across_lanes(
                    lanes[i * TILE : (i + 1) * TILE, :]
                )
            return carry

        lax.fori_loop(0, n_dp // PX, block, 0)

    def close_columns():
        total = jnp.sum(colacc[...], axis=0, keepdims=True)
        colinv[...] = jnp.broadcast_to(1.0 / total, colinv.shape)

    def column_pass():
        colacc[...] = jnp.zeros_like(colacc)

        def step(p, carry):
            scale = down_rows(rowinv[pl.ds(p, 1), :])
            row = pl.ds(pl.multiple_of(p * TILE, TILE), TILE)
            for j in range(tiles):
                lane = slice(j * TILE, (j + 1) * TILE)
                colacc[:, lane] = colacc[:, lane] + fold(code[row, lane].astype(F32) * scale)
            return carry

        lax.fori_loop(0, pairs, step, 0)
        close_columns()

    def row_pass(sweep):
        def step(p, carry):
            row = pl.ds(pl.multiple_of(p * TILE, TILE), TILE)
            total = None
            for j in range(tiles):
                lane = slice(j * TILE, (j + 1) * TILE)
                part = code[row, lane].astype(F32) * colinv[0:1, lane]
                total = part if total is None else total + part
            plane_msg[sweep, me, pl.ds(p, 1), :] = across_lanes(total)
            return carry

        lax.fori_loop(0, pairs, step, 0)

    def reduce_start(sweep):
        size = 2 * pairs if sweep == ITERS - 1 else pairs
        mine = plane_msg.at[sweep, me, pl.ds(0, size)]
        for step in range(1, team):
            send(mine, mine, arp_send.at[sweep, step], arp_recv.at[sweep, step], team_id(step))

    def close_rows(sweep, total):
        rowinv[...] = 1.0 / total[0:pairs]
        if sweep == ITERS - 1:
            norminv[...] = (1.0 / SOFTMAX_TEMPER) / total[pairs : 2 * pairs]

    def reduce_middle(sweep):
        size = 2 * pairs if sweep == ITERS - 1 else pairs
        for step in range(1, team):
            other = plane_msg.at[sweep, lax.rem(me - step + team, team), pl.ds(0, size)]
            arrive(other, arp_send.at[sweep, step], arp_recv.at[sweep, step], team_id(step))
        total = plane_msg[sweep, 0, 0:size, :]
        for other in range(1, team):
            total = total + plane_msg[sweep, other, 0:size, :]
        if direct:
            close_rows(sweep, total)
            return
        line_msg[sweep, z, 0:size, :] = total
        mine = line_msg.at[sweep, z, pl.ds(0, size)]
        for step in range(1, n_blk):
            send(mine, mine, arz_send.at[sweep, step], arz_recv.at[sweep, step], line_id(step))

    def reduce_end(sweep):
        if direct:
            return
        size = 2 * pairs if sweep == ITERS - 1 else pairs
        for step in range(1, n_blk):
            other = line_msg.at[sweep, source(step), pl.ds(0, size)]
            arrive(other, arz_send.at[sweep, step], arz_recv.at[sweep, step], line_id(step))
        total = line_msg[sweep, 0, 0:size, :]
        for other in range(1, n_blk):
            total = total + line_msg[sweep, other, 0:size, :]
        close_rows(sweep, total)

    gather_a(0, rows_a, 0)
    load.wait()
    NC = min(256, cols)

    def normalize(t, carry):
        at = pl.ds(pl.multiple_of(t * NC, NC), NC)
        protos[at, :] = unit_rows(protos[at, :])
        return carry

    lax.fori_loop(0, cols // NC, normalize, 0)
    colacc[...] = jnp.zeros_like(colacc)
    gather_b(0, rows_a, 0)
    for k in range(n_blk):
        if k + 1 < n_blk:
            gather_a(0, rows_a, k + 1)
        if k == n_blk - 1:
            gather_a(1, rows_b, 0)
        gather_c(0, rows_a, k)
        code_group(k)
        if k + 1 < n_blk:
            gather_b(0, rows_a, k + 1)
    close_columns()
    for k in range(1, n_blk):
        gather_a(1, rows_b, k)
        gather_b(1, rows_b, k - 1)
    row_pass(0)
    reduce_start(0)
    gather_b(1, rows_b, n_blk - 1)
    for k in range(n_blk):
        gather_c(1, rows_b, k)

    share = [n_blk * i // 4 for i in range(5)]
    if direct:
        share = [0, n_blk // 2, n_blk // 2, n_blk, n_blk]
    part = 0
    for sweep in range(ITERS):
        if sweep > 0:
            column_pass()
            row_pass(sweep)
            if sweep == ITERS - 1:
                plane_msg[sweep, me, pairs : 2 * pairs, :] = norminv[...]
            reduce_start(sweep)
        if sweep < 2:
            for zi in range(share[part], share[part + 1]):
                pred_group(zi)
            part += 1
        reduce_middle(sweep)
        if sweep < 2:
            for zi in range(share[part], share[part + 1]):
                pred_group(zi)
            part += 1
        reduce_end(sweep)

    def grad_group(zi, slot):
        def rows_step(t, carry):
            p = zi * n_dp + t
            row = pl.ds(pl.multiple_of(p * TILE, TILE), TILE)
            scale = down_rows(rowinv[pl.ds(p, 1), :] * (1.0 / SOFTMAX_TEMPER))
            weight = down_rows(norminv[pl.ds(p, 1), :])
            for j in range(tiles):
                lane = slice(j * TILE, (j + 1) * TILE)
                codes = (code[row, lane].astype(F32) * scale) * colinv[0:1, lane]
                code[row, lane] = (pred[row, lane] * weight - codes).astype(BF16)
            return carry

        lax.fori_loop(0, n_dp, rows_step, 0)

        def dot_step(t, carry):
            xs = t * PX
            size = PX * 2 * hit_dev
            row = pl.multiple_of(zi * group_rows + xs * 2 * hit_dev, size)
            part = jnp.dot(code[pl.ds(row, size), :], protos[...], preferred_element_type=F32)
            for i in range(PX):
                for core in range(2):
                    lo = (i * 2 + core) * hit_dev
                    hits2[slot, core, xs + i] = part[lo : lo + hit_dev, :]
            return carry

        lax.fori_loop(0, n_dp // PX, dot_step, 0)

    SLOTS = hits2.shape[0]
    order = list(range(1, n_blk)) + [0]
    sub_sends = {}
    dp_sends = {}

    def drain(copies):
        for old in copies:
            old.wait_send()
            sends[:] = [copy for copy in sends if copy is not old]

    def scatter_start(i):
        k = order[i]
        slot = i % SLOTS
        if i >= SLOTS:
            drain([sub_sends[i - SLOTS]])
        grad_group(lax.rem(z + k, n_blk), slot)
        sub_sends[i] = send(
            hits2.at[slot, 1 - c], s_in.at[k], rss_send.at[k], rss_recv.at[k], sub_id
        )

    def scatter_sub(i):
        k = order[i]
        slot = i % SLOTS
        arrive(s_in.at[k], rss_send.at[k], rss_recv.at[k], sub_id)
        if i >= SLOTS:
            drain(dp_sends[i - SLOTS])
        red[slot] = hits2[slot, c] + s_in[k]
        dp_sends[i] = []
        for dx in range(1, n_dp):
            other = lax.rem(x + dx, n_dp)
            dp_sends[i].append(
                send(
                    red.at[slot, other],
                    x_in.at[k, dx - 1],
                    rsx_send.at[k, dx],
                    rsx_recv.at[k, dx],
                    {"dp": other},
                )
            )

    def scatter_dp(i):
        k = order[i]
        total = red[i % SLOTS, x]
        for dx in range(1, n_dp):
            other = lax.rem(x + dx, n_dp)
            arrive(x_in.at[k, dx - 1], rsx_send.at[k, dx], rsx_recv.at[k, dx], {"dp": other})
            total = total + x_in[k, dx - 1]
        z_out[k] = total
        if k > 0:
            send(z_out.at[k], z_in.at[k], rsz_send.at[k], rsz_recv.at[k], line_id(k))

    PC = min(512, cols)

    def proto_cols(t, carry):
        lane = pl.ds(pl.multiple_of(t * PC, PC), PC)
        total = None
        for zi in range(n_blk):
            left = code[zi * group_rows : (zi + 1) * group_rows, lane]
            right = rows_b[zi].reshape(group_rows, width)
            part = lax.dot_general(
                left, right, (((0,), (0,)), ((), ())), preferred_element_type=F32
            )
            total = part if total is None else total + part
        gproto_ref[lane, :] = total
        return carry

    for i in range(n_blk):
        scatter_start(i)
        if i >= 1:
            scatter_sub(i - 1)
        if i >= 2:
            scatter_dp(i - 2)
    chunks = cols // PC
    cut = [chunks * i // 4 for i in range(5)]
    lax.fori_loop(cut[0], cut[1], proto_cols, 0)
    scatter_sub(n_blk - 1)
    if n_blk >= 2:
        scatter_dp(n_blk - 2)
    lax.fori_loop(cut[1], cut[2], proto_cols, 0)
    scatter_dp(n_blk - 1)
    lax.fori_loop(cut[2], cut[4], proto_cols, 0)
    total = z_out[0]
    for k in range(1, n_blk):
        arrive(z_in.at[k], rsz_send.at[k], rsz_recv.at[k], line_id(k))
        total = total + z_in[k]
    gview_ref[...] = total
    for copy in sends:
        copy.wait_send()


def kernel_direct(
    n_blk,
    n_dp,
    hit_dev,
    cols,
    region_hbm,
    mask_hbm,
    view_a_hbm,
    view_b_hbm,
    protos_ref,
    gview_ref,
    gproto_ref,
    region_ref,
    mask_ref,
    view_a_ref,
    view_b_ref,
    rows_a,
    rows_b,
    protos,
    code,
    pred,
    lanes,
    colacc,
    colinv,
    rowinv,
    norminv,
    plane_msg,
    norm_msg,
    rowparts,
    scaled,
    hits2,
    red,
    s_in,
    x_in,
    z_out,
    z_in,
    load_sem,
    agz_send,
    agz_recv,
    agx_send,
    agx_recv,
    ags_send,
    ags_recv,
    arp_send,
    arp_recv,
    nrm_send,
    nrm_recv,
    rss_send,
    rss_recv,
    rsx_send,
    rsx_recv,
    rsz_send,
    rsz_recv,
):
    z = lax.axis_index("blk")
    x = lax.axis_index("dp")
    c = lax.axis_index("sub")
    plane = 2 * n_dp
    q = x * 2 + c
    group_rows = plane * hit_dev
    pairs = n_blk * n_dp
    tiles = cols // TILE
    first_tile = (z * plane + q) * tiles
    width = protos.shape[1]
    CC = min(512, cols)
    GC = min(256, cols)
    ctiles = CC // TILE

    barrier = pltpu.get_barrier_semaphore()

    def visit(s):
        room = jnp.minimum(z, n_blk - 1 - z)
        half = (s + 1) // 2
        near = z + half if s % 2 else z - half
        far = jnp.where(2 * z < n_blk - 1, z + (s - room), z - (s - room))
        return jnp.where(s <= 2 * room, near, far)

    near_z = [z] + [visit(s) for s in range(1, n_blk)]
    team = n_blk * plane
    me = z * plane + q

    def team_at(zi, dx, dc):
        xi = lax.rem(x + dx, n_dp)
        ci = 1 - c if dc else c
        return zi * plane + xi * 2 + ci, {"blk": zi, "dp": xi, "sub": ci}

    peers = []
    for s in reversed(range(n_blk)):
        for dx in reversed(range(n_dp)):
            for dc in range(2):
                if s or dx or dc:
                    peers.append(team_at(near_z[s], dx, dc))

    loads = []
    for index, (src, dst) in enumerate(
        (
            (view_a_hbm, view_a_ref),
            (protos_ref.at[pl.ds(q * cols, cols)], protos),
            (view_b_hbm, view_b_ref),
            (region_hbm, region_ref),
            (mask_hbm, mask_ref),
        )
    ):
        load = pltpu.make_async_copy(src, dst, load_sem.at[index])
        load.start()
        loads.append(load)
    for _, device in peers:
        pl.semaphore_signal(barrier, inc=1, device_id=device, device_id_type=MESH)
    loads[0].wait()
    rows_a[z, x, c] = unit_rows(view_a_ref[...])
    loads[2].wait()
    rows_b[z, x, c] = unit_rows(view_b_ref[...])
    pl.semaphore_wait(barrier, team - 1)

    sends = []

    def send(src, dst, send_sem, recv_sem, device):
        copy = pltpu.make_async_remote_copy(
            src_ref=src,
            dst_ref=dst,
            send_sem=send_sem,
            recv_sem=recv_sem,
            device_id=device,
            device_id_type=MESH,
        )
        copy.start()
        sends.append(copy)
        return copy

    def arrive(dst, send_sem, recv_sem, device):
        pltpu.make_async_remote_copy(
            src_ref=dst,
            dst_ref=dst,
            send_sem=send_sem,
            recv_sem=recv_sem,
            device_id=device,
            device_id_type=MESH,
        ).wait_recv()

    sub_id = {"sub": 1 - c}

    def to_sub(v, rows, zi, xi):
        ref = rows.at[zi, xi, c]
        send(ref, ref, ags_send.at[v, zi, xi], ags_recv.at[v, zi, xi], sub_id)

    def to_x(v, rows, zi):
        ref = rows.at[zi, x, c]
        for dx in range(1, n_dp):
            xi = lax.rem(x + dx, n_dp)
            send(ref, ref, agx_send.at[v, zi, xi], agx_recv.at[v, zi, x], {"dp": xi})

    def gather_own(v, rows):
        ref = rows.at[z, x, c]
        for s in reversed(range(1, n_blk)):
            zi = near_z[s]
            send(ref, ref, agz_send.at[v, zi], agz_recv.at[v, z], {"blk": zi})
        to_x(v, rows, z)
        to_sub(v, rows, z, x)

    def gather_z(v, rows, s):
        zi = near_z[s]
        arrive(rows.at[zi, x, c], agz_send.at[v, zi], agz_recv.at[v, zi], {"blk": zi})
        to_x(v, rows, zi)
        to_sub(v, rows, zi, x)

    def gather_x(v, rows, s):
        zi = near_z[s]
        for dx in range(1, n_dp):
            xi = lax.rem(x + n_dp - dx, n_dp)
            arrive(
                rows.at[zi, xi, c], agx_send.at[v, zi, xi], agx_recv.at[v, zi, xi], {"dp": xi}
            )
            to_sub(v, rows, zi, xi)

    def gather_sub(v, rows, s):
        zi = near_z[s]
        for dx in range(n_dp):
            xi = lax.rem(x + dx, n_dp)
            ref = rows.at[zi, xi, 1 - c]
            arrive(ref, ags_send.at[v, zi, xi], ags_recv.at[v, zi, xi], sub_id)

    def bias(pair, core, tile, gain):
        region = region_ref[pair * 2 + core]
        return jnp.where(mask_ref[region, first_tile + tile] > 0, -gain, OFF).astype(F32)

    PX = min(2, n_dp)

    step_rows = PX * 2 * hit_dev
    strips = [(i * hit_dev, i // 2, i % 2) for i in range(PX * 2)]

    def code_group(zi):
        def step(t, carry):
            xs = t * PX
            left = rows_a[zi, pl.ds(xs, PX)].reshape(step_rows, width)
            base = zi * group_rows + xs * 2 * hit_dev
            for c0 in range(0, cols, CC):
                s = lax.dot_general(
                    left,
                    protos[c0 : c0 + CC, :],
                    (((1,), (1,)), ((), ())),
                    preferred_element_type=F32,
                )
                for j in range(ctiles):
                    total = None
                    lane = slice(c0 + j * TILE, c0 + (j + 1) * TILE)
                    for lo, i, core in strips:
                        piece = s[lo : lo + hit_dev, j * TILE : (j + 1) * TILE]
                        b = bias(zi * n_dp + xs + i, core, c0 // TILE + j, CODE_GAIN)
                        e = jnp.exp2(piece * CODE_GAIN + b).astype(BF16)
                        code[pl.ds(pl.multiple_of(base + lo, hit_dev), hit_dev), lane] = e
                        part = fold(e.astype(F32))
                        total = part if total is None else total + part
                    colacc[:, lane] = colacc[:, lane] + total
            return carry

        lax.fori_loop(0, n_dp // PX, step, 0)

    def pred_group(zi):
        def step(t, carry):
            xs = t * PX
            left = rows_b[zi, pl.ds(xs, PX)].reshape(step_rows, width)
            base = zi * group_rows + xs * 2 * hit_dev
            totals = [None] * len(strips)
            for c0 in range(0, cols, CC):
                s = lax.dot_general(
                    left,
                    protos[c0 : c0 + CC, :],
                    (((1,), (1,)), ((), ())),
                    preferred_element_type=F32,
                )
                for n, (lo, i, core) in enumerate(strips):
                    total = None
                    for j in range(ctiles):
                        lane = slice(c0 + j * TILE, c0 + (j + 1) * TILE)
                        piece = s[lo : lo + hit_dev, j * TILE : (j + 1) * TILE]
                        b = bias(zi * n_dp + xs + i, core, c0 // TILE + j, PRED_GAIN)
                        e = jnp.exp2(piece * PRED_GAIN + b)
                        pred[pl.ds(pl.multiple_of(base + lo, hit_dev), hit_dev), lane] = e
                        total = e if total is None else total + e
                    if c0:
                        total = total + lanes[lo : lo + hit_dev, :]
                    lanes[lo : lo + hit_dev, :] = total
            for i in range(PX):
                norm_msg[me, pl.ds(zi * n_dp + xs + i, 1), :] = across_lanes(
                    lanes[i * TILE : (i + 1) * TILE, :]
                )
            return carry

        lax.fori_loop(0, n_dp // PX, step, 0)

    def close_columns(total):
        colinv[...] = jnp.broadcast_to(1.0 / total, colinv.shape)

    def column_pass():
        value = rowinv[...]
        high = value.astype(BF16).astype(F32)
        rest = value - high
        mid = rest.astype(BF16).astype(F32)
        low = rest - mid
        at = lax.broadcasted_iota(jnp.int32, (16, TILE), 0)
        for p in range(pairs):
            block = jnp.where(at == 2, low[p : p + 1, :], 0.0)
            block = jnp.where(at == 1, mid[p : p + 1, :], block)
            block = jnp.where(at == 0, high[p : p + 1, :], block)
            rowparts[:, p * TILE : (p + 1) * TILE] = block.astype(BF16)
        sums = jnp.dot(rowparts[...], code[...], preferred_element_type=F32)
        close_columns(sums[0:1] + sums[1:2] + sums[2:3])

    def row_pass(sweep):
        for p in range(pairs):
            total = None
            for j in range(tiles):
                lane = slice(j * TILE, (j + 1) * TILE)
                part = code[p * TILE : (p + 1) * TILE, lane].astype(F32) * colinv[0:1, lane]
                total = part if total is None else total + part
            plane_msg[sweep, me, p : p + 1, :] = across_lanes(total)

    def share_out(msg, send_sem, recv_sem):
        mine = msg.at[me]
        for other, device in peers:
            send(mine, mine, send_sem.at[other], recv_sem.at[me], device)

    def add_up(msg, send_sem, recv_sem):
        for other, device in reversed(peers):
            arrive(msg.at[other], send_sem.at[other], recv_sem.at[other], device)
        total = msg[0]
        for other in range(1, team):
            total = total + msg[other]
        return total

    def reduce_start(sweep):
        share_out(plane_msg.at[sweep], arp_send.at[sweep], arp_recv.at[sweep])

    def reduce_end(sweep):
        total = add_up(plane_msg.at[sweep], arp_send.at[sweep], arp_recv.at[sweep])
        rowinv[...] = 1.0 / total

    def norm_start():
        share_out(norm_msg, nrm_send, nrm_recv)

    def norm_end():
        total = add_up(norm_msg, nrm_send, nrm_recv)
        norminv[...] = (1.0 / SOFTMAX_TEMPER) / total

    def prepare():
        def step(p, carry):
            row = pl.ds(pl.multiple_of(p * TILE, TILE), TILE)
            weight = down_rows(norminv[pl.ds(p, 1), :])
            for j in range(tiles):
                lane = slice(j * TILE, (j + 1) * TILE)
                scaled[row, lane] = code[row, lane].astype(F32) * colinv[0:1, lane]
                pred[row, lane] = pred[row, lane] * weight
            return carry

        lax.fori_loop(0, pairs, step, 0)

    gather_own(0, rows_a)
    gather_own(1, rows_b)
    loads[1].wait()
    NC = min(256, cols)

    def normalize(t, carry):
        at = pl.ds(pl.multiple_of(t * NC, NC), NC)
        protos[at, :] = unit_rows(protos[at, :])
        return carry

    lax.fori_loop(0, cols // NC, normalize, 0)
    colacc[...] = jnp.zeros_like(colacc)
    loads[3].wait()
    loads[4].wait()
    for s in range(1, n_blk):
        gather_z(0, rows_a, s)
        if s == 1:
            gather_x(0, rows_a, 0)
    gather_sub(0, rows_a, 0)
    code_group(near_z[0])
    for s in range(1, n_blk):
        gather_x(0, rows_a, s)
        if s >= 2:
            gather_sub(0, rows_a, s - 1)
            code_group(near_z[s - 1])
    for s in range(1, n_blk):
        gather_z(1, rows_b, s)
    gather_x(1, rows_b, 0)
    if n_blk > 1:
        gather_sub(0, rows_a, n_blk - 1)
        code_group(near_z[n_blk - 1])
    close_columns(jnp.sum(colacc[...], axis=0, keepdims=True))
    row_pass(0)
    reduce_start(0)
    for s in range(1, n_blk):
        gather_x(1, rows_b, s)
    gather_sub(1, rows_b, 0)
    pred_group(near_z[0])
    reduce_end(0)
    column_pass()
    row_pass(1)
    reduce_start(1)
    for s in range(1, n_blk):
        gather_sub(1, rows_b, s)
        pred_group(near_z[s])
    norm_start()
    reduce_end(1)
    column_pass()
    row_pass(2)
    reduce_start(2)
    norm_end()
    prepare()
    reduce_end(2)

    def grad_group(zi, slot):
        def step(t, carry):
            xs = t * PX
            base = zi * group_rows + xs * 2 * hit_dev
            row = pl.ds(pl.multiple_of(base, step_rows), step_rows)
            scale = jnp.concatenate(
                [
                    down_rows(rowinv[pl.ds(zi * n_dp + xs + i, 1), :] * (1.0 / SOFTMAX_TEMPER))
                    for i in range(PX)
                ],
                axis=0,
            )
            part = None
            for c0 in range(0, cols, GC):
                grads = []
                for j in range(GC // TILE):
                    lane = slice(c0 + j * TILE, c0 + (j + 1) * TILE)
                    grad = (pred[row, lane] - scaled[row, lane] * scale).astype(BF16)
                    code[row, lane] = grad
                    grads.append(grad)
                term = jnp.dot(
                    jnp.concatenate(grads, axis=1),
                    protos[c0 : c0 + GC, :],
                    preferred_element_type=F32,
                )
                part = term if part is None else part + term
            for lo, i, core in strips:
                hits2[slot, core, xs + i] = part[lo : lo + hit_dev, :]
            return carry

        lax.fori_loop(0, n_dp // PX, step, 0)

    SLOTS = hits2.shape[0]
    order = list(reversed(range(n_blk)))
    sub_sends = {}
    dp_sends = {}

    def drain(copies):
        for old in copies:
            old.wait_send()
            sends[:] = [copy for copy in sends if copy is not old]

    def scatter_start(i):
        k = order[i]
        slot = i % SLOTS
        if i >= SLOTS:
            drain([sub_sends[i - SLOTS]])
        grad_group(near_z[k], slot)
        sub_sends[i] = send(
            hits2.at[slot, 1 - c], s_in.at[k], rss_send.at[k], rss_recv.at[k], sub_id
        )

    def scatter_sub(i):
        k = order[i]
        slot = i % SLOTS
        arrive(s_in.at[k], rss_send.at[k], rss_recv.at[k], sub_id)
        if i >= SLOTS:
            drain(dp_sends[i - SLOTS])
        red[slot] = hits2[slot, c] + s_in[k]
        dp_sends[i] = []
        for dx in range(1, n_dp):
            other = lax.rem(x + dx, n_dp)
            dp_sends[i].append(
                send(
                    red.at[slot, other],
                    x_in.at[k, dx - 1],
                    rsx_send.at[k, dx],
                    rsx_recv.at[k, dx],
                    {"dp": other},
                )
            )

    def scatter_dp(i):
        k = order[i]
        total = red[i % SLOTS, x]
        for dx in range(1, n_dp):
            other = lax.rem(x + dx, n_dp)
            arrive(x_in.at[k, dx - 1], rsx_send.at[k, dx], rsx_recv.at[k, dx], {"dp": other})
            total = total + x_in[k, dx - 1]
        z_out[k] = total
        if k > 0:
            zi = near_z[k]
            send(z_out.at[k], z_in.at[z], rsz_send.at[zi], rsz_recv.at[z], {"blk": zi})

    PC = min(512, cols)

    def proto_cols(t, carry):
        lane = pl.ds(pl.multiple_of(t * PC, PC), PC)
        total = None
        for zi in range(n_blk):
            left = code[zi * group_rows : (zi + 1) * group_rows, lane]
            right = rows_b[zi].reshape(group_rows, width)
            part = lax.dot_general(
                left, right, (((0,), (0,)), ((), ())), preferred_element_type=F32
            )
            total = part if total is None else total + part
        gproto_ref[lane, :] = total
        return carry

    for i in range(n_blk):
        scatter_start(i)
        if i >= 1:
            scatter_sub(i - 1)
        if i >= 2:
            scatter_dp(i - 2)
    chunks = cols // PC
    cut = [chunks * i // 4 for i in range(5)]
    lax.fori_loop(cut[0], cut[1], proto_cols, 0)
    scatter_sub(n_blk - 1)
    if n_blk >= 2:
        scatter_dp(n_blk - 2)
    lax.fori_loop(cut[1], cut[2], proto_cols, 0)
    scatter_dp(n_blk - 1)
    lax.fori_loop(cut[2], cut[4], proto_cols, 0)
    total = z_out[0]
    for k in range(1, n_blk):
        zi = near_z[k]
        arrive(z_in.at[zi], rsz_send.at[zi], rsz_recv.at[zi], {"blk": zi})
        total = total + z_in[zi]
    gview_ref[...] = total
    for copy in sends:
        copy.wait_send()


def body_direct(view_a, view_b, prototypes, tile_mask, tile_region):
    n_blk = lax.axis_size("blk")
    n_dp = lax.axis_size("dp")
    hit_dev, width = view_a.shape
    plane = 2 * n_dp
    cols = prototypes.shape[0] // plane
    pairs = n_blk * n_dp
    hits = pairs * 2 * hit_dev
    team = n_blk * plane
    slots = n_blk if n_blk <= 4 else 2
    dma = pltpu.SemaphoreType.DMA
    vmem = pl.BlockSpec(memory_space=pltpu.VMEM)
    anyw = pl.BlockSpec(memory_space=pl.ANY)
    return pl.pallas_call(
        functools.partial(kernel_direct, n_blk, n_dp, hit_dev, cols),
        out_shape=(
            jax.ShapeDtypeStruct((hit_dev, width), F32),
            jax.ShapeDtypeStruct((cols, width), F32),
        ),
        in_specs=[anyw] * 5,
        out_specs=(vmem, vmem),
        scratch_shapes=[
            pltpu.SMEM(tile_region.shape, jnp.int32),
            pltpu.SMEM(tile_mask.shape, jnp.int32),
            pltpu.VMEM((hit_dev, width), BF16),
            pltpu.VMEM((hit_dev, width), BF16),
            pltpu.VMEM((n_blk, n_dp, 2, hit_dev, width), BF16),
            pltpu.VMEM((n_blk, n_dp, 2, hit_dev, width), BF16),
            pltpu.VMEM((cols, width), BF16),
            pltpu.VMEM((hits, cols), BF16),
            pltpu.VMEM((hits, cols), F32),
            pltpu.VMEM((min(2, n_dp) * 2 * hit_dev, TILE), F32),
            pltpu.VMEM((8, cols), F32),
            pltpu.VMEM((8, cols), F32),
            pltpu.VMEM((pairs, TILE), F32),
            pltpu.VMEM((pairs, TILE), F32),
            pltpu.VMEM((ITERS, team, pairs, TILE), F32),
            pltpu.VMEM((team, pairs, TILE), F32),
            pltpu.VMEM((16, hits), BF16),
            pltpu.VMEM((hits, cols), F32),
            pltpu.VMEM((slots, 2, n_dp, hit_dev, width), F32),
            pltpu.VMEM((slots, n_dp, hit_dev, width), F32),
            pltpu.VMEM((n_blk, n_dp, hit_dev, width), F32),
            pltpu.VMEM((n_blk, n_dp - 1, hit_dev, width), F32),
            pltpu.VMEM((n_blk, hit_dev, width), F32),
            pltpu.VMEM((n_blk, hit_dev, width), F32),
            dma((5,)),
            dma((2, n_blk)),
            dma((2, n_blk)),
            dma((2, n_blk, n_dp)),
            dma((2, n_blk, n_dp)),
            dma((2, n_blk, n_dp)),
            dma((2, n_blk, n_dp)),
            dma((ITERS, team)),
            dma((ITERS, team)),
            dma((team,)),
            dma((team,)),
            dma((n_blk,)),
            dma((n_blk,)),
            dma((n_blk, n_dp)),
            dma((n_blk, n_dp)),
            dma((n_blk,)),
            dma((n_blk,)),
        ],
        compiler_params=pltpu.CompilerParams(
            collective_id=0, has_side_effects=True, vmem_limit_bytes=50 << 20
        ),
    )(tile_region, tile_mask, view_a, view_b, prototypes)


def body(view_a, view_b, prototypes, tile_mask, tile_region):
    n_blk = lax.axis_size("blk")
    n_dp = lax.axis_size("dp")
    hit_dev, width = view_a.shape
    plane = 2 * n_dp
    cols = prototypes.shape[0] // plane
    pairs = n_blk * n_dp
    hits = pairs * 2 * hit_dev
    team = n_blk * plane if n_blk * plane <= 16 else plane
    slots = n_blk if n_blk <= 4 else 2
    dma = pltpu.SemaphoreType.DMA
    vmem = pl.BlockSpec(memory_space=pltpu.VMEM)
    smem = pl.BlockSpec(memory_space=pltpu.SMEM)
    return pl.pallas_call(
        functools.partial(kernel, n_blk, n_dp, hit_dev, cols),
        out_shape=(
            jax.ShapeDtypeStruct((hit_dev, width), F32),
            jax.ShapeDtypeStruct((cols, width), F32),
        ),
        in_specs=[smem, smem, vmem, vmem, pl.BlockSpec(memory_space=pl.ANY)],
        out_specs=(vmem, vmem),
        scratch_shapes=[
            pltpu.VMEM((n_blk, n_dp, 2, hit_dev, width), BF16),
            pltpu.VMEM((n_blk, n_dp, 2, hit_dev, width), BF16),
            pltpu.VMEM((cols, width), BF16),
            pltpu.VMEM((hits, cols), BF16),
            pltpu.VMEM((hits, cols), F32),
            pltpu.VMEM((min(2, n_dp) * 2 * hit_dev, TILE), F32),
            pltpu.VMEM((8, cols), F32),
            pltpu.VMEM((8, cols), F32),
            pltpu.VMEM((pairs, TILE), F32),
            pltpu.VMEM((pairs, TILE), F32),
            pltpu.VMEM((ITERS, team, 2 * pairs, TILE), F32),
            pltpu.VMEM((ITERS, n_blk, 2 * pairs, TILE), F32),
            pltpu.VMEM((slots, 2, n_dp, hit_dev, width), F32),
            pltpu.VMEM((slots, n_dp, hit_dev, width), F32),
            pltpu.VMEM((n_blk, n_dp, hit_dev, width), F32),
            pltpu.VMEM((n_blk, n_dp - 1, hit_dev, width), F32),
            pltpu.VMEM((n_blk, hit_dev, width), F32),
            pltpu.VMEM((n_blk, hit_dev, width), F32),
            dma,
            dma((2, n_blk)),
            dma((2, n_blk)),
            dma((2, n_blk, n_dp)),
            dma((2, n_blk, n_dp)),
            dma((2, n_blk, n_dp)),
            dma((2, n_blk, n_dp)),
            dma((ITERS, team)),
            dma((ITERS, team)),
            dma((ITERS, n_blk)),
            dma((ITERS, n_blk)),
            dma((n_blk,)),
            dma((n_blk,)),
            dma((n_blk, n_dp)),
            dma((n_blk, n_dp)),
            dma((n_blk,)),
            dma((n_blk,)),
        ],
        compiler_params=pltpu.CompilerParams(
            collective_id=0, has_side_effects=True, vmem_limit_bytes=(50 if team > plane else 62) << 20
        ),
    )(tile_region, tile_mask, view_a, view_b, prototypes)


def solution(mesh):
    small = mesh.shape["blk"] * mesh.shape["dp"] * mesh.shape["sub"] <= 16
    spread = P(("groups", "blk", "dp", "sub"), None)
    return jax.shard_map(
        body_direct if small else body,
        mesh=mesh,
        in_specs=(spread, spread, P("blk", None), P(), P("groups")),
        out_specs=(spread, spread),
        check_vma=False,
    )
```

```python
import functools
import math

import jax
import jax.numpy as jnp
from jax import lax
from jax.experimental import pallas as pl
from jax.experimental.pallas import tpu as pltpu
from jax.sharding import PartitionSpec as P

TILE = 128
ITERS = 3
SOFTMAX_TEMPER = 0.1
EPSILON = 0.05
LOG2E = math.log2(math.e)
CODE_GAIN = LOG2E / EPSILON
PRED_GAIN = LOG2E / SOFTMAX_TEMPER
OFF = -1e30
MESH = pl.DeviceIdType.MESH
F32 = jnp.float32
BF16 = jnp.bfloat16


def unit_rows(matrix):
    values = matrix.astype(F32)
    return (values * lax.rsqrt(jnp.sum(values * values, axis=1, keepdims=True) + 1e-06)).astype(
        BF16
    )


def down_rows(row):
    return jnp.broadcast_to(row, (TILE, TILE)).T


def across_lanes(block):
    return jnp.sum(block.T, axis=0, keepdims=True)


def fold(block):
    return jnp.sum(block.reshape(block.shape[0] // 8, 8, block.shape[1]), axis=0)


def kernel(
    n_blk,
    n_dp,
    hit_dev,
    cols,
    region_ref,
    mask_ref,
    view_a_ref,
    view_b_ref,
    protos_ref,
    gview_ref,
    gproto_ref,
    rows_a,
    rows_b,
    protos,
    code,
    pred,
    lanes,
    colacc,
    colinv,
    rowinv,
    norminv,
    plane_msg,
    line_msg,
    hits2,
    red,
    s_in,
    x_in,
    z_out,
    z_in,
    load_sem,
    agz_send,
    agz_recv,
    agx_send,
    agx_recv,
    ags_send,
    ags_recv,
    arp_send,
    arp_recv,
    arz_send,
    arz_recv,
    rss_send,
    rss_recv,
    rsx_send,
    rsx_recv,
    rsz_send,
    rsz_recv,
):
    z = lax.axis_index("blk")
    x = lax.axis_index("dp")
    c = lax.axis_index("sub")
    plane = 2 * n_dp
    q = x * 2 + c
    group_rows = plane * hit_dev
    pairs = n_blk * n_dp
    tiles = cols // TILE
    first_tile = (z * plane + q) * tiles
    width = protos.shape[1]
    CC = min(1024, cols)
    ctiles = CC // TILE

    barrier = pltpu.get_barrier_semaphore()

    def plane_id(step):
        other = lax.rem(q + step, plane)
        return {"dp": lax.div(other, 2), "sub": lax.rem(other, 2)}

    def line_id(step):
        return {"blk": lax.rem(z + step, n_blk)}

    direct = n_blk * plane <= 16
    team = n_blk * plane if direct else plane
    me = z * plane + q if direct else q

    def team_id(step):
        if not direct:
            return plane_id(step)
        other = lax.rem(me + step, team)
        return {
            "blk": lax.div(other, plane),
            "dp": lax.rem(lax.div(other, 2), n_dp),
            "sub": lax.rem(other, 2),
        }

    for step in range(1, team):
        pl.semaphore_signal(barrier, inc=1, device_id=team_id(step), device_id_type=MESH)
    if not direct:
        for step in range(1, n_blk):
            pl.semaphore_signal(barrier, inc=1, device_id=line_id(step), device_id_type=MESH)

    load = pltpu.make_async_copy(protos_ref.at[pl.ds(q * cols, cols)], protos, load_sem)
    load.start()
    rows_a[z, x, c] = unit_rows(view_a_ref[...])
    rows_b[z, x, c] = unit_rows(view_b_ref[...])
    pl.semaphore_wait(barrier, team - 1 + (0 if direct else n_blk - 1))

    sends = []

    def send(src, dst, send_sem, recv_sem, device):
        copy = pltpu.make_async_remote_copy(
            src_ref=src,
            dst_ref=dst,
            send_sem=send_sem,
            recv_sem=recv_sem,
            device_id=device,
            device_id_type=MESH,
        )
        copy.start()
        sends.append(copy)
        return copy

    def arrive(dst, send_sem, recv_sem, device):
        pltpu.make_async_remote_copy(
            src_ref=dst,
            dst_ref=dst,
            send_sem=send_sem,
            recv_sem=recv_sem,
            device_id=device,
            device_id_type=MESH,
        ).wait_recv()

    sub_id = {"sub": 1 - c}

    def source(k):
        return lax.rem(z - k + n_blk, n_blk)

    def near(dx):
        return lax.rem(x - dx + n_dp, n_dp)

    def to_sub(v, rows, k, dx):
        ref = rows.at[source(k), near(dx), c]
        send(ref, ref, ags_send.at[v, k, dx], ags_recv.at[v, k, dx], sub_id)

    def gather_a(v, rows, k):
        ref = rows.at[source(k), x, c]
        if k == 0:
            for step in range(1, n_blk):
                send(ref, ref, agz_send.at[v, step], agz_recv.at[v, step], line_id(step))
        else:
            arrive(ref, agz_send.at[v, k], agz_recv.at[v, k], line_id(k))
        for dx in range(1, n_dp):
            send(
                ref,
                ref,
                agx_send.at[v, k, dx],
                agx_recv.at[v, k, dx],
                {"dp": lax.rem(x + dx, n_dp)},
            )
        to_sub(v, rows, k, 0)

    def gather_b(v, rows, k):
        for dx in range(1, n_dp):
            ref = rows.at[source(k), near(dx), c]
            arrive(
                ref,
                agx_send.at[v, k, dx],
                agx_recv.at[v, k, dx],
                {"dp": lax.rem(x + dx, n_dp)},
            )
            to_sub(v, rows, k, dx)

    def gather_c(v, rows, k):
        for dx in range(n_dp):
            ref = rows.at[source(k), near(dx), 1 - c]
            arrive(ref, ags_send.at[v, k, dx], ags_recv.at[v, k, dx], sub_id)

    def bias(pair, core, tile, gain):
        region = region_ref[pair * 2 + core]
        return jnp.where(mask_ref[region, first_tile + tile] > 0, -gain, OFF).astype(F32)

    def score(rows, zi, xs, count, col):
        left = rows[zi, pl.ds(xs, count)].reshape(count * 2 * hit_dev, width)
        right = protos[pl.ds(col, CC), :]
        return lax.dot_general(
            left, right, (((1,), (1,)), ((), ())), preferred_element_type=F32
        )

    PX = min(2, n_dp)

    def code_group(k):
        zi = source(k)

        def step(t, carry):
            xs = (t % (n_dp // PX)) * PX
            ci = t // (n_dp // PX)
            col = pl.multiple_of(ci * CC, CC)
            s = score(rows_a, zi, xs, PX, col)
            for j in range(ctiles):
                total = None
                lane = pl.ds(pl.multiple_of(col + j * TILE, TILE), TILE)
                for i in range(PX):
                    for core in range(2):
                        lo = (i * 2 + core) * hit_dev
                        piece = s[lo : lo + hit_dev, j * TILE : (j + 1) * TILE]
                        b = bias(zi * n_dp + xs + i, core, ci * ctiles + j, CODE_GAIN)
                        e = jnp.exp2(piece * CODE_GAIN + b).astype(BF16)
                        row = pl.multiple_of(zi * group_rows + xs * 2 * hit_dev + lo, hit_dev)
                        code[pl.ds(row, hit_dev), lane] = e
                        part = fold(e.astype(F32))
                        total = part if total is None else total + part
                colacc[:, lane] = colacc[:, lane] + total
            return carry

        lax.fori_loop(0, (n_dp // PX) * (cols // CC), step, 0)

    def pred_group(zi):
        def block(t, carry):
            xs = t * PX
            lanes[...] = jnp.zeros_like(lanes)

            def step(ci, inner):
                col = pl.multiple_of(ci * CC, CC)
                s = score(rows_b, zi, xs, PX, col)
                for i in range(PX):
                    for core in range(2):
                        lo = (i * 2 + core) * hit_dev
                        total = None
                        for j in range(ctiles):
                            piece = s[lo : lo + hit_dev, j * TILE : (j + 1) * TILE]
                            b = bias(zi * n_dp + xs + i, core, ci * ctiles + j, PRED_GAIN)
                            e = jnp.exp2(piece * PRED_GAIN + b)
                            row = pl.multiple_of(
                                zi * group_rows + xs * 2 * hit_dev + lo, hit_dev
                            )
                            lane = pl.ds(pl.multiple_of(col + j * TILE, TILE), TILE)
                            pred[pl.ds(row, hit_dev), lane] = e
                            total = e if total is None else total + e
                        lanes[lo : lo + hit_dev, :] = lanes[lo : lo + hit_dev, :] + total
                return inner

            lax.fori_loop(0, cols // CC, step, 0)
            for i in range(PX):
                norminv[pl.ds(zi * n_dp + xs + i, 1), :] = across_lanes(
                    lanes[i * TILE : (i + 1) * TILE, :]
                )
            return carry

        lax.fori_loop(0, n_dp // PX, block, 0)

    def close_columns():
        total = jnp.sum(colacc[...], axis=0, keepdims=True)
        colinv[...] = jnp.broadcast_to(1.0 / total, colinv.shape)

    def column_pass():
        colacc[...] = jnp.zeros_like(colacc)

        def step(p, carry):
            scale = down_rows(rowinv[pl.ds(p, 1), :])
            row = pl.ds(pl.multiple_of(p * TILE, TILE), TILE)
            for j in range(tiles):
                lane = slice(j * TILE, (j + 1) * TILE)
                colacc[:, lane] = colacc[:, lane] + fold(code[row, lane].astype(F32) * scale)
            return carry

        lax.fori_loop(0, pairs, step, 0)
        close_columns()

    def row_pass(sweep):
        def step(p, carry):
            row = pl.ds(pl.multiple_of(p * TILE, TILE), TILE)
            total = None
            for j in range(tiles):
                lane = slice(j * TILE, (j + 1) * TILE)
                part = code[row, lane].astype(F32) * colinv[0:1, lane]
                total = part if total is None else total + part
            plane_msg[sweep, me, pl.ds(p, 1), :] = across_lanes(total)
            return carry

        lax.fori_loop(0, pairs, step, 0)

    def reduce_start(sweep):
        size = 2 * pairs if sweep == ITERS - 1 else pairs
        mine = plane_msg.at[sweep, me, pl.ds(0, size)]
        for step in range(1, team):
            send(mine, mine, arp_send.at[sweep, step], arp_recv.at[sweep, step], team_id(step))

    def close_rows(sweep, total):
        rowinv[...] = 1.0 / total[0:pairs]
        if sweep == ITERS - 1:
            norminv[...] = (1.0 / SOFTMAX_TEMPER) / total[pairs : 2 * pairs]

    def reduce_middle(sweep):
        size = 2 * pairs if sweep == ITERS - 1 else pairs
        for step in range(1, team):
            other = plane_msg.at[sweep, lax.rem(me - step + team, team), pl.ds(0, size)]
            arrive(other, arp_send.at[sweep, step], arp_recv.at[sweep, step], team_id(step))
        total = plane_msg[sweep, 0, 0:size, :]
        for other in range(1, team):
            total = total + plane_msg[sweep, other, 0:size, :]
        if direct:
            close_rows(sweep, total)
            return
        line_msg[sweep, z, 0:size, :] = total
        mine = line_msg.at[sweep, z, pl.ds(0, size)]
        for step in range(1, n_blk):
            send(mine, mine, arz_send.at[sweep, step], arz_recv.at[sweep, step], line_id(step))

    def reduce_end(sweep):
        if direct:
            return
        size = 2 * pairs if sweep == ITERS - 1 else pairs
        for step in range(1, n_blk):
            other = line_msg.at[sweep, source(step), pl.ds(0, size)]
            arrive(other, arz_send.at[sweep, step], arz_recv.at[sweep, step], line_id(step))
        total = line_msg[sweep, 0, 0:size, :]
        for other in range(1, n_blk):
            total = total + line_msg[sweep, other, 0:size, :]
        close_rows(sweep, total)

    gather_a(0, rows_a, 0)
    load.wait()
    NC = min(256, cols)

    def normalize(t, carry):
        at = pl.ds(pl.multiple_of(t * NC, NC), NC)
        protos[at, :] = unit_rows(protos[at, :])
        return carry

    lax.fori_loop(0, cols // NC, normalize, 0)
    colacc[...] = jnp.zeros_like(colacc)
    gather_b(0, rows_a, 0)
    for k in range(n_blk):
        if k + 1 < n_blk:
            gather_a(0, rows_a, k + 1)
        if k == n_blk - 1:
            gather_a(1, rows_b, 0)
        gather_c(0, rows_a, k)
        code_group(k)
        if k + 1 < n_blk:
            gather_b(0, rows_a, k + 1)
    close_columns()
    for k in range(1, n_blk):
        gather_a(1, rows_b, k)
        gather_b(1, rows_b, k - 1)
    row_pass(0)
    reduce_start(0)
    gather_b(1, rows_b, n_blk - 1)
    for k in range(n_blk):
        gather_c(1, rows_b, k)

    share = [n_blk * i // 4 for i in range(5)]
    if direct:
        share = [0, n_blk // 2, n_blk // 2, n_blk, n_blk]
    part = 0
    for sweep in range(ITERS):
        if sweep > 0:
            column_pass()
            row_pass(sweep)
            if sweep == ITERS - 1:
                plane_msg[sweep, me, pairs : 2 * pairs, :] = norminv[...]
            reduce_start(sweep)
        if sweep < 2:
            for zi in range(share[part], share[part + 1]):
                pred_group(zi)
            part += 1
        reduce_middle(sweep)
        if sweep < 2:
            for zi in range(share[part], share[part + 1]):
                pred_group(zi)
            part += 1
        reduce_end(sweep)

    def grad_group(zi, slot):
        def rows_step(t, carry):
            p = zi * n_dp + t
            row = pl.ds(pl.multiple_of(p * TILE, TILE), TILE)
            scale = down_rows(rowinv[pl.ds(p, 1), :] * (1.0 / SOFTMAX_TEMPER))
            weight = down_rows(norminv[pl.ds(p, 1), :])
            for j in range(tiles):
                lane = slice(j * TILE, (j + 1) * TILE)
                codes = (code[row, lane].astype(F32) * scale) * colinv[0:1, lane]
                code[row, lane] = (pred[row, lane] * weight - codes).astype(BF16)
            return carry

        lax.fori_loop(0, n_dp, rows_step, 0)

        def dot_step(t, carry):
            xs = t * PX
            size = PX * 2 * hit_dev
            row = pl.multiple_of(zi * group_rows + xs * 2 * hit_dev, size)
            part = jnp.dot(code[pl.ds(row, size), :], protos[...], preferred_element_type=F32)
            for i in range(PX):
                for core in range(2):
                    lo = (i * 2 + core) * hit_dev
                    hits2[slot, core, xs + i] = part[lo : lo + hit_dev, :]
            return carry

        lax.fori_loop(0, n_dp // PX, dot_step, 0)

    SLOTS = hits2.shape[0]
    order = list(range(1, n_blk)) + [0]
    sub_sends = {}
    dp_sends = {}

    def drain(copies):
        for old in copies:
            old.wait_send()
            sends[:] = [copy for copy in sends if copy is not old]

    def scatter_start(i):
        k = order[i]
        slot = i % SLOTS
        if i >= SLOTS:
            drain([sub_sends[i - SLOTS]])
        grad_group(lax.rem(z + k, n_blk), slot)
        sub_sends[i] = send(
            hits2.at[slot, 1 - c], s_in.at[k], rss_send.at[k], rss_recv.at[k], sub_id
        )

    def scatter_sub(i):
        k = order[i]
        slot = i % SLOTS
        arrive(s_in.at[k], rss_send.at[k], rss_recv.at[k], sub_id)
        if i >= SLOTS:
            drain(dp_sends[i - SLOTS])
        red[slot] = hits2[slot, c] + s_in[k]
        dp_sends[i] = []
        for dx in range(1, n_dp):
            other = lax.rem(x + dx, n_dp)
            dp_sends[i].append(
                send(
                    red.at[slot, other],
                    x_in.at[k, dx - 1],
                    rsx_send.at[k, dx],
                    rsx_recv.at[k, dx],
                    {"dp": other},
                )
            )

    def scatter_dp(i):
        k = order[i]
        total = red[i % SLOTS, x]
        for dx in range(1, n_dp):
            other = lax.rem(x + dx, n_dp)
            arrive(x_in.at[k, dx - 1], rsx_send.at[k, dx], rsx_recv.at[k, dx], {"dp": other})
            total = total + x_in[k, dx - 1]
        z_out[k] = total
        if k > 0:
            send(z_out.at[k], z_in.at[k], rsz_send.at[k], rsz_recv.at[k], line_id(k))

    PC = min(512, cols)

    def proto_cols(t, carry):
        lane = pl.ds(pl.multiple_of(t * PC, PC), PC)
        total = None
        for zi in range(n_blk):
            left = code[zi * group_rows : (zi + 1) * group_rows, lane]
            right = rows_b[zi].reshape(group_rows, width)
            part = lax.dot_general(
                left, right, (((0,), (0,)), ((), ())), preferred_element_type=F32
            )
            total = part if total is None else total + part
        gproto_ref[lane, :] = total
        return carry

    for i in range(n_blk):
        scatter_start(i)
        if i >= 1:
            scatter_sub(i - 1)
        if i >= 2:
            scatter_dp(i - 2)
    chunks = cols // PC
    cut = [chunks * i // 4 for i in range(5)]
    lax.fori_loop(cut[0], cut[1], proto_cols, 0)
    scatter_sub(n_blk - 1)
    if n_blk >= 2:
        scatter_dp(n_blk - 2)
    lax.fori_loop(cut[1], cut[2], proto_cols, 0)
    scatter_dp(n_blk - 1)
    lax.fori_loop(cut[2], cut[4], proto_cols, 0)
    total = z_out[0]
    for k in range(1, n_blk):
        arrive(z_in.at[k], rsz_send.at[k], rsz_recv.at[k], line_id(k))
        total = total + z_in[k]
    gview_ref[...] = total
    for copy in sends:
        copy.wait_send()


CODE_TOP = 32000.0
SCALE_ROWS = 16


def pack(ref, block):
    rows = block.shape[0]
    top = jnp.max(jnp.abs(block), axis=0, keepdims=True)
    power = jnp.ceil(jnp.log2(jnp.maximum(top, 1e-30)))
    codes = jnp.round(block * (jnp.exp2(-power) * CODE_TOP))
    ref[0:rows, :] = codes.astype(jnp.int32).astype(jnp.int16)
    power = jnp.broadcast_to(power, (SCALE_ROWS, block.shape[1]))
    ref[rows : rows + SCALE_ROWS, :] = power.astype(jnp.int32).astype(jnp.int16)


def unpack(ref):
    rows = ref.shape[0] - SCALE_ROWS
    power = ref[rows : rows + SCALE_ROWS, :].astype(jnp.int32).astype(F32)[0:1]
    return ref[0:rows, :].astype(jnp.int32).astype(F32) * (jnp.exp2(power) * (1.0 / CODE_TOP))


def kernel_direct(
    n_blk,
    n_dp,
    hit_dev,
    cols,
    region_hbm,
    mask_hbm,
    view_a_hbm,
    view_b_hbm,
    protos_ref,
    gview_hbm,
    gproto_hbm,
    gview_ref,
    gproto_ref,
    region_ref,
    mask_ref,
    view_a_ref,
    view_b_ref,
    rows_a,
    rows_b,
    protos,
    code,
    pred,
    lanes,
    colacc,
    colinv,
    rowinv,
    norminv,
    plane_msg,
    norm_msg,
    rowparts,
    scaled,
    hits2,
    red,
    own,
    x_out,
    s_in,
    x_in,
    z_out,
    z_in,
    load_sem,
    agz_send,
    agz_recv,
    agx_send,
    agx_recv,
    ags_send,
    ags_recv,
    arp_send,
    arp_recv,
    nrm_send,
    nrm_recv,
    rss_send,
    rss_recv,
    rsx_send,
    rsx_recv,
    rsz_send,
    rsz_recv,
):
    z = lax.axis_index("blk")
    x = lax.axis_index("dp")
    c = lax.axis_index("sub")
    plane = 2 * n_dp
    q = x * 2 + c
    group_rows = plane * hit_dev
    pairs = n_blk * n_dp
    tiles = cols // TILE
    first_tile = (z * plane + q) * tiles
    width = protos.shape[1]
    CC = min(512, cols)
    GC = min(256, cols)
    ctiles = CC // TILE

    barrier = pltpu.get_barrier_semaphore()

    def visit(s):
        room = jnp.minimum(z, n_blk - 1 - z)
        half = (s + 1) // 2
        near = z + half if s % 2 else z - half
        far = jnp.where(2 * z < n_blk - 1, z + (s - room), z - (s - room))
        return jnp.where(s <= 2 * room, near, far)

    near_z = [z] + [visit(s) for s in range(1, n_blk)]
    team = n_blk * plane
    me = z * plane + q

    def team_at(zi, dx, dc):
        xi = lax.rem(x + dx, n_dp)
        ci = 1 - c if dc else c
        return zi * plane + xi * 2 + ci, {"blk": zi, "dp": xi, "sub": ci}

    peers = []
    for s in reversed(range(n_blk)):
        for dx in reversed(range(n_dp)):
            for dc in range(2):
                if s or dx or dc:
                    peers.append(team_at(near_z[s], dx, dc))

    loads = []
    for index, (src, dst) in enumerate(
        (
            (view_a_hbm, view_a_ref),
            (protos_ref.at[pl.ds(q * cols, cols)], protos),
            (view_b_hbm, view_b_ref),
            (region_hbm, region_ref),
            (mask_hbm, mask_ref),
        )
    ):
        load = pltpu.make_async_copy(src, dst, load_sem.at[index])
        load.start()
        loads.append(load)
    for _, device in peers:
        pl.semaphore_signal(barrier, inc=1, device_id=device, device_id_type=MESH)
    loads[0].wait()
    rows_a[z, x, c] = unit_rows(view_a_ref[...])
    loads[2].wait()
    rows_b[z, x, c] = unit_rows(view_b_ref[...])
    pl.semaphore_wait(barrier, team - 1)

    sends = []

    def send(src, dst, send_sem, recv_sem, device):
        copy = pltpu.make_async_remote_copy(
            src_ref=src,
            dst_ref=dst,
            send_sem=send_sem,
            recv_sem=recv_sem,
            device_id=device,
            device_id_type=MESH,
        )
        copy.start()
        sends.append(copy)
        return copy

    def arrive(dst, send_sem, recv_sem, device):
        pltpu.make_async_remote_copy(
            src_ref=dst,
            dst_ref=dst,
            send_sem=send_sem,
            recv_sem=recv_sem,
            device_id=device,
            device_id_type=MESH,
        ).wait_recv()

    sub_id = {"sub": 1 - c}

    def to_sub(v, rows, zi, xi):
        ref = rows.at[zi, xi, c]
        send(ref, ref, ags_send.at[v, zi, xi], ags_recv.at[v, zi, xi], sub_id)

    def to_x(v, rows, zi):
        ref = rows.at[zi, x, c]
        for dx in range(1, n_dp):
            xi = lax.rem(x + dx, n_dp)
            send(ref, ref, agx_send.at[v, zi, xi], agx_recv.at[v, zi, x], {"dp": xi})

    def gather_own(v, rows):
        ref = rows.at[z, x, c]
        for s in reversed(range(1, n_blk)):
            zi = near_z[s]
            send(ref, ref, agz_send.at[v, zi], agz_recv.at[v, z], {"blk": zi})
        to_x(v, rows, z)
        to_sub(v, rows, z, x)

    def gather_z(v, rows, s):
        zi = near_z[s]
        arrive(rows.at[zi, x, c], agz_send.at[v, zi], agz_recv.at[v, zi], {"blk": zi})
        to_x(v, rows, zi)
        to_sub(v, rows, zi, x)

    def gather_x(v, rows, s):
        zi = near_z[s]
        for dx in range(1, n_dp):
            xi = lax.rem(x + n_dp - dx, n_dp)
            arrive(
                rows.at[zi, xi, c], agx_send.at[v, zi, xi], agx_recv.at[v, zi, xi], {"dp": xi}
            )
            to_sub(v, rows, zi, xi)

    def gather_sub(v, rows, s):
        zi = near_z[s]
        for dx in range(n_dp):
            xi = lax.rem(x + dx, n_dp)
            ref = rows.at[zi, xi, 1 - c]
            arrive(ref, ags_send.at[v, zi, xi], ags_recv.at[v, zi, xi], sub_id)

    def bias(pair, core, tile, gain):
        region = region_ref[pair * 2 + core]
        return jnp.where(mask_ref[region, first_tile + tile] > 0, -gain, OFF).astype(F32)

    PX = min(2, n_dp)

    step_rows = PX * 2 * hit_dev
    strips = [(i * hit_dev, i // 2, i % 2) for i in range(PX * 2)]

    def code_group(zi):
        def step(t, carry):
            xs = t * PX
            left = rows_a[zi, pl.ds(xs, PX)].reshape(step_rows, width)
            base = zi * group_rows + xs * 2 * hit_dev
            for c0 in range(0, cols, CC):
                s = lax.dot_general(
                    left,
                    protos[c0 : c0 + CC, :],
                    (((1,), (1,)), ((), ())),
                    preferred_element_type=F32,
                )
                for j in range(ctiles):
                    total = None
                    lane = slice(c0 + j * TILE, c0 + (j + 1) * TILE)
                    for lo, i, core in strips:
                        piece = s[lo : lo + hit_dev, j * TILE : (j + 1) * TILE]
                        b = bias(zi * n_dp + xs + i, core, c0 // TILE + j, CODE_GAIN)
                        e = jnp.exp2(piece * CODE_GAIN + b).astype(BF16)
                        code[pl.ds(pl.multiple_of(base + lo, hit_dev), hit_dev), lane] = e
                        part = fold(e.astype(F32))
                        total = part if total is None else total + part
                    colacc[:, lane] = colacc[:, lane] + total
            return carry

        lax.fori_loop(0, n_dp // PX, step, 0)

    def pred_group(zi):
        def step(t, carry):
            xs = t * PX
            left = rows_b[zi, pl.ds(xs, PX)].reshape(step_rows, width)
            base = zi * group_rows + xs * 2 * hit_dev
            totals = [None] * len(strips)
            for c0 in range(0, cols, CC):
                s = lax.dot_general(
                    left,
                    protos[c0 : c0 + CC, :],
                    (((1,), (1,)), ((), ())),
                    preferred_element_type=F32,
                )
                for n, (lo, i, core) in enumerate(strips):
                    total = None
                    for j in range(ctiles):
                        lane = slice(c0 + j * TILE, c0 + (j + 1) * TILE)
                        piece = s[lo : lo + hit_dev, j * TILE : (j + 1) * TILE]
                        b = bias(zi * n_dp + xs + i, core, c0 // TILE + j, PRED_GAIN)
                        e = jnp.exp2(piece * PRED_GAIN + b)
                        pred[pl.ds(pl.multiple_of(base + lo, hit_dev), hit_dev), lane] = e
                        total = e if total is None else total + e
                    if c0:
                        total = total + lanes[lo : lo + hit_dev, :]
                    lanes[lo : lo + hit_dev, :] = total
            for i in range(PX):
                norm_msg[me, pl.ds(zi * n_dp + xs + i, 1), :] = across_lanes(
                    lanes[i * TILE : (i + 1) * TILE, :]
                )
            return carry

        lax.fori_loop(0, n_dp // PX, step, 0)

    def close_columns(total):
        colinv[...] = jnp.broadcast_to(1.0 / total, colinv.shape)

    def column_pass():
        value = rowinv[...]
        high = value.astype(BF16).astype(F32)
        rest = value - high
        mid = rest.astype(BF16).astype(F32)
        low = rest - mid
        at = lax.broadcasted_iota(jnp.int32, (16, TILE), 0)
        for p in range(pairs):
            block = jnp.where(at == 2, low[p : p + 1, :], 0.0)
            block = jnp.where(at == 1, mid[p : p + 1, :], block)
            block = jnp.where(at == 0, high[p : p + 1, :], block)
            rowparts[:, p * TILE : (p + 1) * TILE] = block.astype(BF16)
        sums = jnp.dot(rowparts[...], code[...], preferred_element_type=F32)
        close_columns(sums[0:1] + sums[1:2] + sums[2:3])

    def row_pass(sweep):
        for p in range(pairs):
            total = None
            for j in range(tiles):
                lane = slice(j * TILE, (j + 1) * TILE)
                part = code[p * TILE : (p + 1) * TILE, lane].astype(F32) * colinv[0:1, lane]
                total = part if total is None else total + part
            plane_msg[sweep, me, p : p + 1, :] = across_lanes(total)

    def share_out(msg, send_sem, recv_sem):
        mine = msg.at[me]
        for other, device in peers:
            send(mine, mine, send_sem.at[other], recv_sem.at[me], device)

    def add_up(msg, send_sem, recv_sem):
        for other, device in reversed(peers):
            arrive(msg.at[other], send_sem.at[other], recv_sem.at[other], device)
        total = msg[0]
        for other in range(1, team):
            total = total + msg[other]
        return total

    def reduce_start(sweep):
        share_out(plane_msg.at[sweep], arp_send.at[sweep], arp_recv.at[sweep])

    def reduce_end(sweep):
        total = add_up(plane_msg.at[sweep], arp_send.at[sweep], arp_recv.at[sweep])
        rowinv[...] = 1.0 / total

    def norm_start():
        share_out(norm_msg, nrm_send, nrm_recv)

    def norm_end():
        total = add_up(norm_msg, nrm_send, nrm_recv)
        norminv[...] = (1.0 / SOFTMAX_TEMPER) / total

    def prepare():
        def step(p, carry):
            row = pl.ds(pl.multiple_of(p * TILE, TILE), TILE)
            weight = down_rows(norminv[pl.ds(p, 1), :])
            for j in range(tiles):
                lane = slice(j * TILE, (j + 1) * TILE)
                scaled[row, lane] = code[row, lane].astype(F32) * colinv[0:1, lane]
                pred[row, lane] = pred[row, lane] * weight
            return carry

        lax.fori_loop(0, pairs, step, 0)

    gather_own(0, rows_a)
    gather_own(1, rows_b)
    loads[1].wait()
    NC = min(256, cols)

    def normalize(t, carry):
        at = pl.ds(pl.multiple_of(t * NC, NC), NC)
        protos[at, :] = unit_rows(protos[at, :])
        return carry

    lax.fori_loop(0, cols // NC, normalize, 0)
    colacc[...] = jnp.zeros_like(colacc)
    loads[3].wait()
    loads[4].wait()
    for s in range(1, n_blk):
        gather_z(0, rows_a, s)
        if s == 1:
            gather_x(0, rows_a, 0)
    gather_sub(0, rows_a, 0)
    code_group(near_z[0])
    for s in range(1, n_blk):
        gather_x(0, rows_a, s)
        if s >= 2:
            gather_sub(0, rows_a, s - 1)
            code_group(near_z[s - 1])
    for s in range(1, n_blk):
        gather_z(1, rows_b, s)
    gather_x(1, rows_b, 0)
    if n_blk > 1:
        gather_sub(0, rows_a, n_blk - 1)
        code_group(near_z[n_blk - 1])
    close_columns(jnp.sum(colacc[...], axis=0, keepdims=True))
    row_pass(0)
    reduce_start(0)
    for s in range(1, n_blk):
        gather_x(1, rows_b, s)
    gather_sub(1, rows_b, 0)
    pred_group(near_z[0])
    reduce_end(0)
    column_pass()
    row_pass(1)
    reduce_start(1)
    for s in range(1, n_blk):
        gather_sub(1, rows_b, s)
        pred_group(near_z[s])
    norm_start()
    reduce_end(1)
    column_pass()
    row_pass(2)
    reduce_start(2)
    norm_end()
    prepare()
    reduce_end(2)

    def grad_group(zi, slot):
        def step(t, carry):
            xs = t * PX
            base = zi * group_rows + xs * 2 * hit_dev
            row = pl.ds(pl.multiple_of(base, step_rows), step_rows)
            scale = jnp.concatenate(
                [
                    down_rows(rowinv[pl.ds(zi * n_dp + xs + i, 1), :] * (1.0 / SOFTMAX_TEMPER))
                    for i in range(PX)
                ],
                axis=0,
            )
            part = None
            for c0 in range(0, cols, GC):
                grads = []
                for j in range(GC // TILE):
                    lane = slice(c0 + j * TILE, c0 + (j + 1) * TILE)
                    grad = (pred[row, lane] - scaled[row, lane] * scale).astype(BF16)
                    code[row, lane] = grad
                    grads.append(grad)
                term = jnp.dot(
                    jnp.concatenate(grads, axis=1),
                    protos[c0 : c0 + GC, :],
                    preferred_element_type=F32,
                )
                part = term if part is None else part + term
            for lo, i, core in strips:
                hits2[slot, core, xs + i] = part[lo : lo + hit_dev, :]
            return carry

        lax.fori_loop(0, n_dp // PX, step, 0)

    SLOTS = hits2.shape[0]
    order = list(reversed(range(n_blk)))
    sub_sends = {}
    dp_sends = {}

    def drain(copies):
        for old in copies:
            old.wait_send()
            sends[:] = [copy for copy in sends if copy is not old]

    def scatter_start(i):
        k = order[i]
        slot = i % SLOTS
        if i >= SLOTS:
            drain([sub_sends[i - SLOTS]])
        grad_group(near_z[k], slot)
        sub_sends[i] = send(
            hits2.at[slot, 1 - c], s_in.at[k], rss_send.at[k], rss_recv.at[k], sub_id
        )

    def scatter_sub(i):
        k = order[i]
        slot = i % SLOTS
        arrive(s_in.at[k], rss_send.at[k], rss_recv.at[k], sub_id)
        if i >= SLOTS:
            drain(dp_sends[i - SLOTS])
        dp_sends[i] = []
        for dx in range(1, n_dp):
            other = lax.rem(x + dx, n_dp)
            block = hits2[slot, c, other] + s_in[k, other]
            pack(x_out.at[slot, dx - 1], block)
            dp_sends[i].append(
                send(
                    x_out.at[slot, dx - 1],
                    x_in.at[k, dx - 1],
                    rsx_send.at[k, dx],
                    rsx_recv.at[k, dx],
                    {"dp": other},
                )
            )
        red[slot] = hits2[slot, c, x] + s_in[k, x]

    def scatter_dp(i):
        k = order[i]
        total = red[i % SLOTS]
        for dx in range(1, n_dp):
            other = lax.rem(x + dx, n_dp)
            arrive(x_in.at[k, dx - 1], rsx_send.at[k, dx], rsx_recv.at[k, dx], {"dp": other})
            total = total + unpack(x_in.at[k, dx - 1])
        if k > 0:
            zi = near_z[k]
            pack(z_out.at[k - 1], total)
            send(z_out.at[k - 1], z_in.at[z], rsz_send.at[zi], rsz_recv.at[z], {"blk": zi})
        else:
            own[...] = total

    PC = min(512, cols)

    def proto_cols(t, carry):
        lane = pl.ds(pl.multiple_of(t * PC, PC), PC)
        total = None
        for zi in range(n_blk):
            left = code[zi * group_rows : (zi + 1) * group_rows, lane]
            right = rows_b[zi].reshape(group_rows, width)
            part = lax.dot_general(
                left, right, (((0,), (0,)), ((), ())), preferred_element_type=F32
            )
            total = part if total is None else total + part
        gproto_ref[lane, :] = total
        return carry

    for i in range(n_blk):
        scatter_start(i)
        if i >= 1:
            scatter_sub(i - 1)
        if i >= 2:
            scatter_dp(i - 2)
    chunks = cols // PC
    cut = [chunks * i // 4 for i in range(5)]
    lax.fori_loop(cut[0], cut[1], proto_cols, 0)
    scatter_sub(n_blk - 1)
    if n_blk >= 2:
        scatter_dp(n_blk - 2)
    lax.fori_loop(cut[1], cut[2], proto_cols, 0)
    scatter_dp(n_blk - 1)
    lax.fori_loop(cut[2], cut[4], proto_cols, 0)
    stores = [pltpu.make_async_copy(gproto_ref, gproto_hbm, load_sem.at[5])]
    stores[0].start()
    total = own[...]
    for k in range(1, n_blk):
        zi = near_z[k]
        arrive(z_in.at[zi], rsz_send.at[zi], rsz_recv.at[zi], {"blk": zi})
        total = total + unpack(z_in.at[zi])
    gview_ref[...] = total
    stores.append(pltpu.make_async_copy(gview_ref, gview_hbm, load_sem.at[6]))
    stores[1].start()
    for copy in stores:
        copy.wait()
    for copy in sends:
        copy.wait_send()


def store(gview_ref, gproto_ref, gview_out, gproto_out, held, sem, out_sem):
    rows = gview_ref.shape[0]
    parts = 8
    size = gproto_ref.shape[0] // parts
    spans = [(gview_ref, gview_out, held.at[pl.ds(0, rows)])]
    for i in range(parts):
        at = pl.ds(i * size, size)
        spans.append((gproto_ref.at[at], gproto_out.at[at], held.at[pl.ds(rows + i * size, size)]))
    ins = [pltpu.make_async_copy(a, h, sem.at[i]) for i, (a, b, h) in enumerate(spans)]
    outs = [pltpu.make_async_copy(h, b, out_sem.at[i]) for i, (a, b, h) in enumerate(spans)]
    for copy in ins:
        copy.start()
    for copy, out in zip(ins, outs):
        copy.wait()
        out.start()
    for out in outs:
        out.wait()


def body_direct(view_a, view_b, prototypes, tile_mask, tile_region):
    n_blk = lax.axis_size("blk")
    n_dp = lax.axis_size("dp")
    hit_dev, width = view_a.shape
    plane = 2 * n_dp
    cols = prototypes.shape[0] // plane
    pairs = n_blk * n_dp
    hits = pairs * 2 * hit_dev
    team = n_blk * plane
    slots = n_blk if n_blk <= 4 else 2
    dma = pltpu.SemaphoreType.DMA
    vmem = pl.BlockSpec(memory_space=pltpu.VMEM)
    hbm = pl.BlockSpec(memory_space=pltpu.HBM)
    grads = pl.pallas_call(
        functools.partial(kernel_direct, n_blk, n_dp, hit_dev, cols),
        out_shape=(
            jax.ShapeDtypeStruct((hit_dev, width), F32),
            jax.ShapeDtypeStruct((cols, width), F32),
        ),
        in_specs=[hbm] * 5,
        out_specs=(hbm, hbm),
        scratch_shapes=[
            pltpu.VMEM((hit_dev, width), F32),
            pltpu.VMEM((cols, width), F32),
            pltpu.SMEM(tile_region.shape, jnp.int32),
            pltpu.SMEM(tile_mask.shape, jnp.int32),
            pltpu.VMEM((hit_dev, width), BF16),
            pltpu.VMEM((hit_dev, width), BF16),
            pltpu.VMEM((n_blk, n_dp, 2, hit_dev, width), BF16),
            pltpu.VMEM((n_blk, n_dp, 2, hit_dev, width), BF16),
            pltpu.VMEM((cols, width), BF16),
            pltpu.VMEM((hits, cols), BF16),
            pltpu.VMEM((hits, cols), F32),
            pltpu.VMEM((min(2, n_dp) * 2 * hit_dev, TILE), F32),
            pltpu.VMEM((8, cols), F32),
            pltpu.VMEM((8, cols), F32),
            pltpu.VMEM((pairs, TILE), F32),
            pltpu.VMEM((pairs, TILE), F32),
            pltpu.VMEM((ITERS, team, pairs, TILE), F32),
            pltpu.VMEM((team, pairs, TILE), F32),
            pltpu.VMEM((16, hits), BF16),
            pltpu.VMEM((hits, cols), F32),
            pltpu.VMEM((slots, 2, n_dp, hit_dev, width), F32),
            pltpu.VMEM((slots, hit_dev, width), F32),
            pltpu.VMEM((hit_dev, width), F32),
            pltpu.VMEM((slots, max(n_dp - 1, 1), hit_dev + SCALE_ROWS, width), jnp.int16),
            pltpu.VMEM((n_blk, n_dp, hit_dev, width), F32),
            pltpu.VMEM((n_blk, max(n_dp - 1, 1), hit_dev + SCALE_ROWS, width), jnp.int16),
            pltpu.VMEM((n_blk, hit_dev + SCALE_ROWS, width), jnp.int16),
            pltpu.VMEM((n_blk, hit_dev + SCALE_ROWS, width), jnp.int16),
            dma((7,)),
            dma((2, n_blk)),
            dma((2, n_blk)),
            dma((2, n_blk, n_dp)),
            dma((2, n_blk, n_dp)),
            dma((2, n_blk, n_dp)),
            dma((2, n_blk, n_dp)),
            dma((ITERS, team)),
            dma((ITERS, team)),
            dma((team,)),
            dma((team,)),
            dma((n_blk,)),
            dma((n_blk,)),
            dma((n_blk, n_dp)),
            dma((n_blk, n_dp)),
            dma((n_blk,)),
            dma((n_blk,)),
        ],
        compiler_params=pltpu.CompilerParams(
            collective_id=0, has_side_effects=True, vmem_limit_bytes=(64 << 20)
        ),
    )(tile_region, tile_mask, view_a, view_b, prototypes)
    return pl.pallas_call(
        store,
        out_shape=(
            jax.ShapeDtypeStruct((hit_dev, width), F32),
            jax.ShapeDtypeStruct((cols, width), F32),
        ),
        in_specs=[hbm] * 2,
        out_specs=[hbm] * 2,
        scratch_shapes=[pltpu.VMEM((hit_dev + cols, width), F32), dma((9,)), dma((9,))],
        compiler_params=pltpu.CompilerParams(vmem_limit_bytes=64 << 20),
    )(*grads)


def body(view_a, view_b, prototypes, tile_mask, tile_region):
    n_blk = lax.axis_size("blk")
    n_dp = lax.axis_size("dp")
    hit_dev, width = view_a.shape
    plane = 2 * n_dp
    cols = prototypes.shape[0] // plane
    pairs = n_blk * n_dp
    hits = pairs * 2 * hit_dev
    team = n_blk * plane if n_blk * plane <= 16 else plane
    slots = n_blk if n_blk <= 4 else 2
    dma = pltpu.SemaphoreType.DMA
    vmem = pl.BlockSpec(memory_space=pltpu.VMEM)
    smem = pl.BlockSpec(memory_space=pltpu.SMEM)
    return pl.pallas_call(
        functools.partial(kernel, n_blk, n_dp, hit_dev, cols),
        out_shape=(
            jax.ShapeDtypeStruct((hit_dev, width), F32),
            jax.ShapeDtypeStruct((cols, width), F32),
        ),
        in_specs=[smem, smem, vmem, vmem, pl.BlockSpec(memory_space=pl.ANY)],
        out_specs=(vmem, vmem),
        scratch_shapes=[
            pltpu.VMEM((n_blk, n_dp, 2, hit_dev, width), BF16),
            pltpu.VMEM((n_blk, n_dp, 2, hit_dev, width), BF16),
            pltpu.VMEM((cols, width), BF16),
            pltpu.VMEM((hits, cols), BF16),
            pltpu.VMEM((hits, cols), F32),
            pltpu.VMEM((min(2, n_dp) * 2 * hit_dev, TILE), F32),
            pltpu.VMEM((8, cols), F32),
            pltpu.VMEM((8, cols), F32),
            pltpu.VMEM((pairs, TILE), F32),
            pltpu.VMEM((pairs, TILE), F32),
            pltpu.VMEM((ITERS, team, 2 * pairs, TILE), F32),
            pltpu.VMEM((ITERS, n_blk, 2 * pairs, TILE), F32),
            pltpu.VMEM((slots, 2, n_dp, hit_dev, width), F32),
            pltpu.VMEM((slots, n_dp, hit_dev, width), F32),
            pltpu.VMEM((n_blk, n_dp, hit_dev, width), F32),
            pltpu.VMEM((n_blk, n_dp - 1, hit_dev, width), F32),
            pltpu.VMEM((n_blk, hit_dev, width), F32),
            pltpu.VMEM((n_blk, hit_dev, width), F32),
            dma,
            dma((2, n_blk)),
            dma((2, n_blk)),
            dma((2, n_blk, n_dp)),
            dma((2, n_blk, n_dp)),
            dma((2, n_blk, n_dp)),
            dma((2, n_blk, n_dp)),
            dma((ITERS, team)),
            dma((ITERS, team)),
            dma((ITERS, n_blk)),
            dma((ITERS, n_blk)),
            dma((n_blk,)),
            dma((n_blk,)),
            dma((n_blk, n_dp)),
            dma((n_blk, n_dp)),
            dma((n_blk,)),
            dma((n_blk,)),
        ],
        compiler_params=pltpu.CompilerParams(
            collective_id=0, has_side_effects=True, vmem_limit_bytes=(50 if team > plane else 62) << 20
        ),
    )(tile_region, tile_mask, view_a, view_b, prototypes)


def solution(mesh):
    small = mesh.shape["blk"] * mesh.shape["dp"] * mesh.shape["sub"] <= 16
    spread = P(("groups", "blk", "dp", "sub"), None)
    return jax.shard_map(
        body_direct if small else body,
        mesh=mesh,
        in_specs=(spread, spread, P("blk", None), P(), P("groups")),
        out_specs=(spread, spread),
        check_vma=False,
    )
```

```python
import functools
import math

import jax
import jax.numpy as jnp
from jax import lax
from jax.experimental import pallas as pl
from jax.experimental.pallas import tpu as pltpu
from jax.sharding import PartitionSpec as P

TILE = 128
ITERS = 3
SOFTMAX_TEMPER = 0.1
EPSILON = 0.05
LOG2E = math.log2(math.e)
CODE_GAIN = LOG2E / EPSILON
PRED_GAIN = LOG2E / SOFTMAX_TEMPER
OFF = -1e30
MESH = pl.DeviceIdType.MESH
F32 = jnp.float32
BF16 = jnp.bfloat16


def unit_rows(matrix):
    values = matrix.astype(F32)
    return (values * lax.rsqrt(jnp.sum(values * values, axis=1, keepdims=True) + 1e-06)).astype(
        BF16
    )


def down_rows(row):
    return jnp.broadcast_to(row, (TILE, TILE)).T


def across_lanes(block):
    return jnp.sum(block.T, axis=0, keepdims=True)


def fold(block):
    return jnp.sum(block.reshape(block.shape[0] // 8, 8, block.shape[1]), axis=0)


def kernel(
    n_blk,
    n_dp,
    hit_dev,
    cols,
    region_ref,
    mask_ref,
    view_a_ref,
    view_b_ref,
    protos_ref,
    gview_ref,
    gproto_ref,
    rows_a,
    rows_b,
    protos,
    code,
    pred,
    lanes,
    colacc,
    colinv,
    rowinv,
    norminv,
    plane_msg,
    line_msg,
    hits2,
    red,
    s_in,
    x_in,
    z_out,
    z_in,
    load_sem,
    agz_send,
    agz_recv,
    agx_send,
    agx_recv,
    ags_send,
    ags_recv,
    arp_send,
    arp_recv,
    arz_send,
    arz_recv,
    rss_send,
    rss_recv,
    rsx_send,
    rsx_recv,
    rsz_send,
    rsz_recv,
):
    z = lax.axis_index("blk")
    x = lax.axis_index("dp")
    c = lax.axis_index("sub")
    plane = 2 * n_dp
    q = x * 2 + c
    group_rows = plane * hit_dev
    pairs = n_blk * n_dp
    tiles = cols // TILE
    first_tile = (z * plane + q) * tiles
    width = protos.shape[1]
    CC = min(1024, cols)
    ctiles = CC // TILE

    barrier = pltpu.get_barrier_semaphore()

    def plane_id(step):
        other = lax.rem(q + step, plane)
        return {"dp": lax.div(other, 2), "sub": lax.rem(other, 2)}

    def line_id(step):
        return {"blk": lax.rem(z + step, n_blk)}

    direct = n_blk * plane <= 16
    team = n_blk * plane if direct else plane
    me = z * plane + q if direct else q

    def team_id(step):
        if not direct:
            return plane_id(step)
        other = lax.rem(me + step, team)
        return {
            "blk": lax.div(other, plane),
            "dp": lax.rem(lax.div(other, 2), n_dp),
            "sub": lax.rem(other, 2),
        }

    for step in range(1, team):
        pl.semaphore_signal(barrier, inc=1, device_id=team_id(step), device_id_type=MESH)
    if not direct:
        for step in range(1, n_blk):
            pl.semaphore_signal(barrier, inc=1, device_id=line_id(step), device_id_type=MESH)

    load = pltpu.make_async_copy(protos_ref.at[pl.ds(q * cols, cols)], protos, load_sem)
    load.start()
    rows_a[z, x, c] = unit_rows(view_a_ref[...])
    rows_b[z, x, c] = unit_rows(view_b_ref[...])
    pl.semaphore_wait(barrier, team - 1 + (0 if direct else n_blk - 1))

    sends = []

    def send(src, dst, send_sem, recv_sem, device):
        copy = pltpu.make_async_remote_copy(
            src_ref=src,
            dst_ref=dst,
            send_sem=send_sem,
            recv_sem=recv_sem,
            device_id=device,
            device_id_type=MESH,
        )
        copy.start()
        sends.append(copy)
        return copy

    def arrive(dst, send_sem, recv_sem, device):
        pltpu.make_async_remote_copy(
            src_ref=dst,
            dst_ref=dst,
            send_sem=send_sem,
            recv_sem=recv_sem,
            device_id=device,
            device_id_type=MESH,
        ).wait_recv()

    sub_id = {"sub": 1 - c}

    def source(k):
        return lax.rem(z - k + n_blk, n_blk)

    def near(dx):
        return lax.rem(x - dx + n_dp, n_dp)

    def to_sub(v, rows, k, dx):
        ref = rows.at[source(k), near(dx), c]
        send(ref, ref, ags_send.at[v, k, dx], ags_recv.at[v, k, dx], sub_id)

    def gather_a(v, rows, k):
        ref = rows.at[source(k), x, c]
        if k == 0:
            for step in range(1, n_blk):
                send(ref, ref, agz_send.at[v, step], agz_recv.at[v, step], line_id(step))
        else:
            arrive(ref, agz_send.at[v, k], agz_recv.at[v, k], line_id(k))
        for dx in range(1, n_dp):
            send(
                ref,
                ref,
                agx_send.at[v, k, dx],
                agx_recv.at[v, k, dx],
                {"dp": lax.rem(x + dx, n_dp)},
            )
        to_sub(v, rows, k, 0)

    def gather_b(v, rows, k):
        for dx in range(1, n_dp):
            ref = rows.at[source(k), near(dx), c]
            arrive(
                ref,
                agx_send.at[v, k, dx],
                agx_recv.at[v, k, dx],
                {"dp": lax.rem(x + dx, n_dp)},
            )
            to_sub(v, rows, k, dx)

    def gather_c(v, rows, k):
        for dx in range(n_dp):
            ref = rows.at[source(k), near(dx), 1 - c]
            arrive(ref, ags_send.at[v, k, dx], ags_recv.at[v, k, dx], sub_id)

    def bias(pair, core, tile, gain):
        region = region_ref[pair * 2 + core]
        return jnp.where(mask_ref[region, first_tile + tile] > 0, -gain, OFF).astype(F32)

    def score(rows, zi, xs, count, col):
        left = rows[zi, pl.ds(xs, count)].reshape(count * 2 * hit_dev, width)
        right = protos[pl.ds(col, CC), :]
        return lax.dot_general(
            left, right, (((1,), (1,)), ((), ())), preferred_element_type=F32
        )

    PX = min(2, n_dp)

    def code_group(k):
        zi = source(k)

        def step(t, carry):
            xs = (t % (n_dp // PX)) * PX
            ci = t // (n_dp // PX)
            col = pl.multiple_of(ci * CC, CC)
            s = score(rows_a, zi, xs, PX, col)
            for j in range(ctiles):
                total = None
                lane = pl.ds(pl.multiple_of(col + j * TILE, TILE), TILE)
                for i in range(PX):
                    for core in range(2):
                        lo = (i * 2 + core) * hit_dev
                        piece = s[lo : lo + hit_dev, j * TILE : (j + 1) * TILE]
                        b = bias(zi * n_dp + xs + i, core, ci * ctiles + j, CODE_GAIN)
                        e = jnp.exp2(piece * CODE_GAIN + b).astype(BF16)
                        row = pl.multiple_of(zi * group_rows + xs * 2 * hit_dev + lo, hit_dev)
                        code[pl.ds(row, hit_dev), lane] = e
                        part = fold(e.astype(F32))
                        total = part if total is None else total + part
                colacc[:, lane] = colacc[:, lane] + total
            return carry

        lax.fori_loop(0, (n_dp // PX) * (cols // CC), step, 0)

    def pred_group(zi):
        def block(t, carry):
            xs = t * PX
            lanes[...] = jnp.zeros_like(lanes)

            def step(ci, inner):
                col = pl.multiple_of(ci * CC, CC)
                s = score(rows_b, zi, xs, PX, col)
                for i in range(PX):
                    for core in range(2):
                        lo = (i * 2 + core) * hit_dev
                        total = None
                        for j in range(ctiles):
                            piece = s[lo : lo + hit_dev, j * TILE : (j + 1) * TILE]
                            b = bias(zi * n_dp + xs + i, core, ci * ctiles + j, PRED_GAIN)
                            e = jnp.exp2(piece * PRED_GAIN + b)
                            row = pl.multiple_of(
                                zi * group_rows + xs * 2 * hit_dev + lo, hit_dev
                            )
                            lane = pl.ds(pl.multiple_of(col + j * TILE, TILE), TILE)
                            pred[pl.ds(row, hit_dev), lane] = e
                            total = e if total is None else total + e
                        lanes[lo : lo + hit_dev, :] = lanes[lo : lo + hit_dev, :] + total
                return inner

            lax.fori_loop(0, cols // CC, step, 0)
            for i in range(PX):
                norminv[pl.ds(zi * n_dp + xs + i, 1), :] = across_lanes(
                    lanes[i * TILE : (i + 1) * TILE, :]
                )
            return carry

        lax.fori_loop(0, n_dp // PX, block, 0)

    def close_columns():
        total = jnp.sum(colacc[...], axis=0, keepdims=True)
        colinv[...] = jnp.broadcast_to(1.0 / total, colinv.shape)

    def column_pass():
        colacc[...] = jnp.zeros_like(colacc)

        def step(p, carry):
            scale = down_rows(rowinv[pl.ds(p, 1), :])
            row = pl.ds(pl.multiple_of(p * TILE, TILE), TILE)
            for j in range(tiles):
                lane = slice(j * TILE, (j + 1) * TILE)
                colacc[:, lane] = colacc[:, lane] + fold(code[row, lane].astype(F32) * scale)
            return carry

        lax.fori_loop(0, pairs, step, 0)
        close_columns()

    def row_pass(sweep):
        def step(p, carry):
            row = pl.ds(pl.multiple_of(p * TILE, TILE), TILE)
            total = None
            for j in range(tiles):
                lane = slice(j * TILE, (j + 1) * TILE)
                part = code[row, lane].astype(F32) * colinv[0:1, lane]
                total = part if total is None else total + part
            plane_msg[sweep, me, pl.ds(p, 1), :] = across_lanes(total)
            return carry

        lax.fori_loop(0, pairs, step, 0)

    def reduce_start(sweep):
        size = 2 * pairs if sweep == ITERS - 1 else pairs
        mine = plane_msg.at[sweep, me, pl.ds(0, size)]
        for step in range(1, team):
            send(mine, mine, arp_send.at[sweep, step], arp_recv.at[sweep, step], team_id(step))

    def close_rows(sweep, total):
        rowinv[...] = 1.0 / total[0:pairs]
        if sweep == ITERS - 1:
            norminv[...] = (1.0 / SOFTMAX_TEMPER) / total[pairs : 2 * pairs]

    def reduce_middle(sweep):
        size = 2 * pairs if sweep == ITERS - 1 else pairs
        for step in range(1, team):
            other = plane_msg.at[sweep, lax.rem(me - step + team, team), pl.ds(0, size)]
            arrive(other, arp_send.at[sweep, step], arp_recv.at[sweep, step], team_id(step))
        total = plane_msg[sweep, 0, 0:size, :]
        for other in range(1, team):
            total = total + plane_msg[sweep, other, 0:size, :]
        if direct:
            close_rows(sweep, total)
            return
        line_msg[sweep, z, 0:size, :] = total
        mine = line_msg.at[sweep, z, pl.ds(0, size)]
        for step in range(1, n_blk):
            send(mine, mine, arz_send.at[sweep, step], arz_recv.at[sweep, step], line_id(step))

    def reduce_end(sweep):
        if direct:
            return
        size = 2 * pairs if sweep == ITERS - 1 else pairs
        for step in range(1, n_blk):
            other = line_msg.at[sweep, source(step), pl.ds(0, size)]
            arrive(other, arz_send.at[sweep, step], arz_recv.at[sweep, step], line_id(step))
        total = line_msg[sweep, 0, 0:size, :]
        for other in range(1, n_blk):
            total = total + line_msg[sweep, other, 0:size, :]
        close_rows(sweep, total)

    gather_a(0, rows_a, 0)
    load.wait()
    NC = min(256, cols)

    def normalize(t, carry):
        at = pl.ds(pl.multiple_of(t * NC, NC), NC)
        protos[at, :] = unit_rows(protos[at, :])
        return carry

    lax.fori_loop(0, cols // NC, normalize, 0)
    colacc[...] = jnp.zeros_like(colacc)
    gather_b(0, rows_a, 0)
    for k in range(n_blk):
        if k + 1 < n_blk:
            gather_a(0, rows_a, k + 1)
        if k == n_blk - 1:
            gather_a(1, rows_b, 0)
        gather_c(0, rows_a, k)
        code_group(k)
        if k + 1 < n_blk:
            gather_b(0, rows_a, k + 1)
    close_columns()
    for k in range(1, n_blk):
        gather_a(1, rows_b, k)
        gather_b(1, rows_b, k - 1)
    row_pass(0)
    reduce_start(0)
    gather_b(1, rows_b, n_blk - 1)
    for k in range(n_blk):
        gather_c(1, rows_b, k)

    share = [n_blk * i // 4 for i in range(5)]
    if direct:
        share = [0, n_blk // 2, n_blk // 2, n_blk, n_blk]
    part = 0
    for sweep in range(ITERS):
        if sweep > 0:
            column_pass()
            row_pass(sweep)
            if sweep == ITERS - 1:
                plane_msg[sweep, me, pairs : 2 * pairs, :] = norminv[...]
            reduce_start(sweep)
        if sweep < 2:
            for zi in range(share[part], share[part + 1]):
                pred_group(zi)
            part += 1
        reduce_middle(sweep)
        if sweep < 2:
            for zi in range(share[part], share[part + 1]):
                pred_group(zi)
            part += 1
        reduce_end(sweep)

    def grad_group(zi, slot):
        def rows_step(t, carry):
            p = zi * n_dp + t
            row = pl.ds(pl.multiple_of(p * TILE, TILE), TILE)
            scale = down_rows(rowinv[pl.ds(p, 1), :] * (1.0 / SOFTMAX_TEMPER))
            weight = down_rows(norminv[pl.ds(p, 1), :])
            for j in range(tiles):
                lane = slice(j * TILE, (j + 1) * TILE)
                codes = (code[row, lane].astype(F32) * scale) * colinv[0:1, lane]
                code[row, lane] = (pred[row, lane] * weight - codes).astype(BF16)
            return carry

        lax.fori_loop(0, n_dp, rows_step, 0)

        def dot_step(t, carry):
            xs = t * PX
            size = PX * 2 * hit_dev
            row = pl.multiple_of(zi * group_rows + xs * 2 * hit_dev, size)
            part = jnp.dot(code[pl.ds(row, size), :], protos[...], preferred_element_type=F32)
            for i in range(PX):
                for core in range(2):
                    lo = (i * 2 + core) * hit_dev
                    hits2[slot, core, xs + i] = part[lo : lo + hit_dev, :]
            return carry

        lax.fori_loop(0, n_dp // PX, dot_step, 0)

    SLOTS = hits2.shape[0]
    order = list(range(1, n_blk)) + [0]
    sub_sends = {}
    dp_sends = {}

    def drain(copies):
        for old in copies:
            old.wait_send()
            sends[:] = [copy for copy in sends if copy is not old]

    def scatter_start(i):
        k = order[i]
        slot = i % SLOTS
        if i >= SLOTS:
            drain([sub_sends[i - SLOTS]])
        grad_group(lax.rem(z + k, n_blk), slot)
        sub_sends[i] = send(
            hits2.at[slot, 1 - c], s_in.at[k], rss_send.at[k], rss_recv.at[k], sub_id
        )

    def scatter_sub(i):
        k = order[i]
        slot = i % SLOTS
        arrive(s_in.at[k], rss_send.at[k], rss_recv.at[k], sub_id)
        if i >= SLOTS:
            drain(dp_sends[i - SLOTS])
        red[slot] = hits2[slot, c] + s_in[k]
        dp_sends[i] = []
        for dx in range(1, n_dp):
            other = lax.rem(x + dx, n_dp)
            dp_sends[i].append(
                send(
                    red.at[slot, other],
                    x_in.at[k, dx - 1],
                    rsx_send.at[k, dx],
                    rsx_recv.at[k, dx],
                    {"dp": other},
                )
            )

    def scatter_dp(i):
        k = order[i]
        total = red[i % SLOTS, x]
        for dx in range(1, n_dp):
            other = lax.rem(x + dx, n_dp)
            arrive(x_in.at[k, dx - 1], rsx_send.at[k, dx], rsx_recv.at[k, dx], {"dp": other})
            total = total + x_in[k, dx - 1]
        z_out[k] = total
        if k > 0:
            send(z_out.at[k], z_in.at[k], rsz_send.at[k], rsz_recv.at[k], line_id(k))

    PC = min(512, cols)

    def proto_cols(t, carry):
        lane = pl.ds(pl.multiple_of(t * PC, PC), PC)
        total = None
        for zi in range(n_blk):
            left = code[zi * group_rows : (zi + 1) * group_rows, lane]
            right = rows_b[zi].reshape(group_rows, width)
            part = lax.dot_general(
                left, right, (((0,), (0,)), ((), ())), preferred_element_type=F32
            )
            total = part if total is None else total + part
        gproto_ref[lane, :] = total
        return carry

    for i in range(n_blk):
        scatter_start(i)
        if i >= 1:
            scatter_sub(i - 1)
        if i >= 2:
            scatter_dp(i - 2)
    chunks = cols // PC
    cut = [chunks * i // 4 for i in range(5)]
    lax.fori_loop(cut[0], cut[1], proto_cols, 0)
    scatter_sub(n_blk - 1)
    if n_blk >= 2:
        scatter_dp(n_blk - 2)
    lax.fori_loop(cut[1], cut[2], proto_cols, 0)
    scatter_dp(n_blk - 1)
    lax.fori_loop(cut[2], cut[4], proto_cols, 0)
    total = z_out[0]
    for k in range(1, n_blk):
        arrive(z_in.at[k], rsz_send.at[k], rsz_recv.at[k], line_id(k))
        total = total + z_in[k]
    gview_ref[...] = total
    for copy in sends:
        copy.wait_send()


CODE_TOP = 32000.0
SCALE_ROWS = 16


def pack(ref, block):
    rows = block.shape[0]
    top = jnp.max(jnp.abs(block), axis=0, keepdims=True)
    power = jnp.ceil(jnp.log2(jnp.maximum(top, 1e-30)))
    codes = jnp.round(block * (jnp.exp2(-power) * CODE_TOP))
    ref[0:rows, :] = codes.astype(jnp.int32).astype(jnp.int16)
    power = jnp.broadcast_to(power, (SCALE_ROWS, block.shape[1]))
    ref[rows : rows + SCALE_ROWS, :] = power.astype(jnp.int32).astype(jnp.int16)


def unpack(ref):
    rows = ref.shape[0] - SCALE_ROWS
    power = ref[rows : rows + SCALE_ROWS, :].astype(jnp.int32).astype(F32)[0:1]
    return ref[0:rows, :].astype(jnp.int32).astype(F32) * (jnp.exp2(power) * (1.0 / CODE_TOP))


def kernel_direct(
    n_blk,
    n_dp,
    hit_dev,
    cols,
    region_hbm,
    mask_hbm,
    view_a_hbm,
    view_b_hbm,
    protos_ref,
    gview_hbm,
    gproto_hbm,
    gview_ref,
    gproto_ref,
    region_ref,
    mask_ref,
    view_a_ref,
    view_b_ref,
    rows_a,
    rows_b,
    protos,
    code,
    pred,
    lanes,
    colacc,
    colinv,
    rowinv,
    norminv,
    plane_msg,
    norm_msg,
    rowparts,
    scaled,
    hits2,
    red,
    own,
    x_out,
    s_in,
    x_in,
    z_out,
    z_in,
    load_sem,
    agz_send,
    agz_recv,
    agx_send,
    agx_recv,
    ags_send,
    ags_recv,
    arp_send,
    arp_recv,
    nrm_send,
    nrm_recv,
    rss_send,
    rss_recv,
    rsx_send,
    rsx_recv,
    rsz_send,
    rsz_recv,
):
    z = lax.axis_index("blk")
    x = lax.axis_index("dp")
    c = lax.axis_index("sub")
    plane = 2 * n_dp
    q = x * 2 + c
    group_rows = plane * hit_dev
    pairs = n_blk * n_dp
    tiles = cols // TILE
    first_tile = (z * plane + q) * tiles
    width = protos.shape[1]
    CC = min(512, cols)
    GC = min(256, cols)
    ctiles = CC // TILE

    barrier = pltpu.get_barrier_semaphore()

    def visit(s):
        room = jnp.minimum(z, n_blk - 1 - z)
        half = (s + 1) // 2
        near = z + half if s % 2 else z - half
        far = jnp.where(2 * z < n_blk - 1, z + (s - room), z - (s - room))
        return jnp.where(s <= 2 * room, near, far)

    near_z = [z] + [visit(s) for s in range(1, n_blk)]
    team = n_blk * plane
    me = z * plane + q

    def team_at(zi, dx, dc):
        xi = lax.rem(x + dx, n_dp)
        ci = 1 - c if dc else c
        return zi * plane + xi * 2 + ci, {"blk": zi, "dp": xi, "sub": ci}

    peers = []
    for s in reversed(range(n_blk)):
        for dx in reversed(range(n_dp)):
            for dc in range(2):
                if s or dx or dc:
                    peers.append(team_at(near_z[s], dx, dc))

    loads = []
    for index, (src, dst) in enumerate(
        (
            (view_a_hbm, view_a_ref),
            (protos_ref.at[pl.ds(q * cols, cols)], protos),
            (view_b_hbm, view_b_ref),
            (region_hbm, region_ref),
            (mask_hbm, mask_ref),
        )
    ):
        load = pltpu.make_async_copy(src, dst, load_sem.at[index])
        load.start()
        loads.append(load)
    for _, device in peers:
        pl.semaphore_signal(barrier, inc=1, device_id=device, device_id_type=MESH)
    loads[0].wait()
    rows_a[z, x, c] = unit_rows(view_a_ref[...])
    pl.semaphore_wait(barrier, team - 1)

    sends = []

    def send(src, dst, send_sem, recv_sem, device):
        copy = pltpu.make_async_remote_copy(
            src_ref=src,
            dst_ref=dst,
            send_sem=send_sem,
            recv_sem=recv_sem,
            device_id=device,
            device_id_type=MESH,
        )
        copy.start()
        sends.append(copy)
        return copy

    def arrive(dst, send_sem, recv_sem, device):
        pltpu.make_async_remote_copy(
            src_ref=dst,
            dst_ref=dst,
            send_sem=send_sem,
            recv_sem=recv_sem,
            device_id=device,
            device_id_type=MESH,
        ).wait_recv()

    sub_id = {"sub": 1 - c}

    def to_sub(v, rows, zi, xi):
        ref = rows.at[zi, xi, c]
        send(ref, ref, ags_send.at[v, zi, xi], ags_recv.at[v, zi, xi], sub_id)

    def to_x(v, rows, zi):
        ref = rows.at[zi, x, c]
        for dx in range(1, n_dp):
            xi = lax.rem(x + dx, n_dp)
            send(ref, ref, agx_send.at[v, zi, xi], agx_recv.at[v, zi, x], {"dp": xi})

    def gather_own(v, rows):
        ref = rows.at[z, x, c]
        for s in reversed(range(1, n_blk)):
            zi = near_z[s]
            send(ref, ref, agz_send.at[v, zi], agz_recv.at[v, z], {"blk": zi})
        to_x(v, rows, z)
        to_sub(v, rows, z, x)

    def gather_z(v, rows, s):
        zi = near_z[s]
        arrive(rows.at[zi, x, c], agz_send.at[v, zi], agz_recv.at[v, zi], {"blk": zi})
        to_x(v, rows, zi)
        to_sub(v, rows, zi, x)

    def gather_x(v, rows, s):
        zi = near_z[s]
        for dx in range(1, n_dp):
            xi = lax.rem(x + n_dp - dx, n_dp)
            arrive(
                rows.at[zi, xi, c], agx_send.at[v, zi, xi], agx_recv.at[v, zi, xi], {"dp": xi}
            )
            to_sub(v, rows, zi, xi)

    def gather_sub(v, rows, s, dx):
        zi = near_z[s]
        xi = lax.rem(x + dx, n_dp)
        ref = rows.at[zi, xi, 1 - c]
        arrive(ref, ags_send.at[v, zi, xi], ags_recv.at[v, zi, xi], sub_id)

    def bias(pair, core, tile, gain):
        region = region_ref[pair * 2 + core]
        return jnp.where(mask_ref[region, first_tile + tile] > 0, -gain, OFF).astype(F32)

    PX = min(2, n_dp)

    step_rows = PX * 2 * hit_dev
    strips = [(i * hit_dev, i // 2, i % 2) for i in range(PX * 2)]

    def code_block(zi, xi):
        left = rows_a[zi, xi].reshape(TILE, width)
        base = zi * group_rows + xi * TILE
        pair = zi * n_dp + xi

        def step(t, carry):
            c0 = pl.multiple_of(t * CC, CC)
            s = lax.dot_general(
                left,
                protos[pl.ds(c0, CC), :],
                (((1,), (1,)), ((), ())),
                preferred_element_type=F32,
            )
            for j in range(ctiles):
                total = None
                lane = pl.ds(pl.multiple_of(c0 + j * TILE, TILE), TILE)
                for core in range(2):
                    lo = core * hit_dev
                    piece = s[lo : lo + hit_dev, j * TILE : (j + 1) * TILE]
                    b = bias(pair, core, t * ctiles + j, CODE_GAIN)
                    e = jnp.exp2(piece * CODE_GAIN + b).astype(BF16)
                    code[pl.ds(pl.multiple_of(base + lo, hit_dev), hit_dev), lane] = e
                    part = fold(e.astype(F32))
                    total = part if total is None else total + part
                colacc[:, lane] = colacc[:, lane] + total
            return carry

        lax.fori_loop(0, cols // CC, step, 0, unroll=True)

    def code_half(s, dx):
        gather_sub(0, rows_a, s, dx)
        code_block(near_z[s], lax.rem(x + dx, n_dp))

    def pred_group(zi):
        def step(t, carry):
            xs = t * PX
            left = rows_b[zi, pl.ds(xs, PX)].reshape(step_rows, width)
            base = zi * group_rows + xs * 2 * hit_dev
            totals = [None] * len(strips)
            for c0 in range(0, cols, CC):
                s = lax.dot_general(
                    left,
                    protos[c0 : c0 + CC, :],
                    (((1,), (1,)), ((), ())),
                    preferred_element_type=F32,
                )
                for n, (lo, i, core) in enumerate(strips):
                    total = None
                    for j in range(ctiles):
                        lane = slice(c0 + j * TILE, c0 + (j + 1) * TILE)
                        piece = s[lo : lo + hit_dev, j * TILE : (j + 1) * TILE]
                        b = bias(zi * n_dp + xs + i, core, c0 // TILE + j, PRED_GAIN)
                        e = jnp.exp2(piece * PRED_GAIN + b)
                        pred[pl.ds(pl.multiple_of(base + lo, hit_dev), hit_dev), lane] = e
                        total = e if total is None else total + e
                    if c0:
                        total = total + lanes[lo : lo + hit_dev, :]
                    lanes[lo : lo + hit_dev, :] = total
            for i in range(PX):
                norm_msg[me, pl.ds(zi * n_dp + xs + i, 1), :] = across_lanes(
                    lanes[i * TILE : (i + 1) * TILE, :]
                )
            return carry

        lax.fori_loop(0, n_dp // PX, step, 0)

    def close_columns(total):
        colinv[...] = jnp.broadcast_to(1.0 / total, colinv.shape)

    def column_pass():
        value = rowinv[...]
        high = value.astype(BF16).astype(F32)
        rest = value - high
        mid = rest.astype(BF16).astype(F32)
        low = rest - mid
        at = lax.broadcasted_iota(jnp.int32, (16, TILE), 0)
        for p in range(pairs):
            block = jnp.where(at == 2, low[p : p + 1, :], 0.0)
            block = jnp.where(at == 1, mid[p : p + 1, :], block)
            block = jnp.where(at == 0, high[p : p + 1, :], block)
            rowparts[:, p * TILE : (p + 1) * TILE] = block.astype(BF16)
        sums = jnp.dot(rowparts[...], code[...], preferred_element_type=F32)
        close_columns(sums[0:1] + sums[1:2] + sums[2:3])

    def row_pass(sweep):
        for p in range(pairs):
            total = None
            for j in range(tiles):
                lane = slice(j * TILE, (j + 1) * TILE)
                part = code[p * TILE : (p + 1) * TILE, lane].astype(F32) * colinv[0:1, lane]
                total = part if total is None else total + part
            plane_msg[sweep, me, p : p + 1, :] = across_lanes(total)

    def share_out(msg, send_sem, recv_sem):
        mine = msg.at[me]
        for other, device in peers:
            send(mine, mine, send_sem.at[other], recv_sem.at[me], device)

    def add_up(msg, send_sem, recv_sem):
        for other, device in reversed(peers):
            arrive(msg.at[other], send_sem.at[other], recv_sem.at[other], device)
        total = msg[0]
        for other in range(1, team):
            total = total + msg[other]
        return total

    def reduce_start(sweep):
        share_out(plane_msg.at[sweep], arp_send.at[sweep], arp_recv.at[sweep])

    def reduce_end(sweep):
        total = add_up(plane_msg.at[sweep], arp_send.at[sweep], arp_recv.at[sweep])
        rowinv[...] = 1.0 / total

    def norm_start():
        share_out(norm_msg, nrm_send, nrm_recv)

    def norm_end():
        total = add_up(norm_msg, nrm_send, nrm_recv)
        norminv[...] = (1.0 / SOFTMAX_TEMPER) / total

    def prepare():
        def step(p, carry):
            row = pl.ds(pl.multiple_of(p * TILE, TILE), TILE)
            weight = down_rows(norminv[pl.ds(p, 1), :])
            for j in range(tiles):
                lane = slice(j * TILE, (j + 1) * TILE)
                scaled[row, lane] = code[row, lane].astype(F32) * colinv[0:1, lane]
                pred[row, lane] = pred[row, lane] * weight
            return carry

        lax.fori_loop(0, pairs, step, 0)

    gather_own(0, rows_a)
    loads[1].wait()
    NC = min(256, cols)

    def normalize(t, carry):
        at = pl.ds(pl.multiple_of(t * NC, NC), NC)
        protos[at, :] = unit_rows(protos[at, :])
        return carry

    lax.fori_loop(0, cols // NC, normalize, 0)
    colacc[...] = jnp.zeros_like(colacc)
    loads[3].wait()
    loads[4].wait()
    others = range(1, n_dp)
    for s in range(1, n_blk):
        gather_z(0, rows_a, s)
        if s == 1:
            gather_x(0, rows_a, 0)
        if s == min(2, n_blk - 1):
            for dx in range(n_dp):
                code_half(0, dx)
    loads[2].wait()
    rows_b[z, x, c] = unit_rows(view_b_ref[...])
    gather_own(1, rows_b)
    for s in range(1, n_blk - 1):
        code_half(s, 0)
    for s in range(1, n_blk - 1):
        gather_x(0, rows_a, s)
    code_half(n_blk - 1, 0)
    for dx in others:
        code_half(1, dx)
    gather_x(0, rows_a, n_blk - 1)
    for s in range(2, n_blk - 1):
        for dx in others:
            code_half(s, dx)
    gather_x(1, rows_b, 0)
    for dx in others:
        code_half(n_blk - 1, dx)
    close_columns(jnp.sum(colacc[...], axis=0, keepdims=True))
    row_pass(0)
    reduce_start(0)
    for s in range(1, n_blk):
        gather_z(1, rows_b, s)
    for dx in range(n_dp):
        gather_sub(1, rows_b, 0, dx)
    pred_group(near_z[0])
    reduce_end(0)
    column_pass()
    row_pass(1)
    reduce_start(1)
    for s in range(1, n_blk):
        gather_x(1, rows_b, s)
    for s in range(1, n_blk):
        for dx in range(n_dp):
            gather_sub(1, rows_b, s, dx)
        pred_group(near_z[s])
    norm_start()
    reduce_end(1)
    column_pass()
    row_pass(2)
    reduce_start(2)
    norm_end()
    prepare()
    reduce_end(2)

    def grad_group(zi, slot):
        def step(t, carry):
            xs = t * PX
            base = zi * group_rows + xs * 2 * hit_dev
            row = pl.ds(pl.multiple_of(base, step_rows), step_rows)
            scale = jnp.concatenate(
                [
                    down_rows(rowinv[pl.ds(zi * n_dp + xs + i, 1), :] * (1.0 / SOFTMAX_TEMPER))
                    for i in range(PX)
                ],
                axis=0,
            )
            part = None
            for c0 in range(0, cols, GC):
                grads = []
                for j in range(GC // TILE):
                    lane = slice(c0 + j * TILE, c0 + (j + 1) * TILE)
                    grad = (pred[row, lane] - scaled[row, lane] * scale).astype(BF16)
                    code[row, lane] = grad
                    grads.append(grad)
                term = jnp.dot(
                    jnp.concatenate(grads, axis=1),
                    protos[c0 : c0 + GC, :],
                    preferred_element_type=F32,
                )
                part = term if part is None else part + term
            for lo, i, core in strips:
                hits2[slot, core, xs + i] = part[lo : lo + hit_dev, :]
            return carry

        lax.fori_loop(0, n_dp // PX, step, 0)

    SLOTS = hits2.shape[0]
    order = list(reversed(range(n_blk)))
    sub_sends = {}
    dp_sends = {}

    def drain(copies):
        for old in copies:
            old.wait_send()
            sends[:] = [copy for copy in sends if copy is not old]

    def scatter_start(i):
        k = order[i]
        slot = i % SLOTS
        if i >= SLOTS:
            drain([sub_sends[i - SLOTS]])
        grad_group(near_z[k], slot)
        sub_sends[i] = send(
            hits2.at[slot, 1 - c], s_in.at[k], rss_send.at[k], rss_recv.at[k], sub_id
        )

    def scatter_sub(i):
        k = order[i]
        slot = i % SLOTS
        arrive(s_in.at[k], rss_send.at[k], rss_recv.at[k], sub_id)
        if i >= SLOTS:
            drain(dp_sends[i - SLOTS])
        dp_sends[i] = []
        for dx in range(1, n_dp):
            other = lax.rem(x + dx, n_dp)
            block = hits2[slot, c, other] + s_in[k, other]
            pack(x_out.at[slot, dx - 1], block)
            dp_sends[i].append(
                send(
                    x_out.at[slot, dx - 1],
                    x_in.at[k, dx - 1],
                    rsx_send.at[k, dx],
                    rsx_recv.at[k, dx],
                    {"dp": other},
                )
            )
        red[slot] = hits2[slot, c, x] + s_in[k, x]

    def scatter_dp(i):
        k = order[i]
        total = red[i % SLOTS]
        for dx in range(1, n_dp):
            other = lax.rem(x + dx, n_dp)
            arrive(x_in.at[k, dx - 1], rsx_send.at[k, dx], rsx_recv.at[k, dx], {"dp": other})
            total = total + unpack(x_in.at[k, dx - 1])
        if k > 0:
            zi = near_z[k]
            pack(z_out.at[k - 1], total)
            send(z_out.at[k - 1], z_in.at[z], rsz_send.at[zi], rsz_recv.at[z], {"blk": zi})
        else:
            own[...] = total

    PC = min(512, cols)

    def proto_cols(t, carry):
        lane = pl.ds(pl.multiple_of(t * PC, PC), PC)
        total = None
        for zi in range(n_blk):
            left = code[zi * group_rows : (zi + 1) * group_rows, lane]
            right = rows_b[zi].reshape(group_rows, width)
            part = lax.dot_general(
                left, right, (((0,), (0,)), ((), ())), preferred_element_type=F32
            )
            total = part if total is None else total + part
        gproto_ref[lane, :] = total
        return carry

    for i in range(n_blk):
        scatter_start(i)
        if i >= 1:
            scatter_sub(i - 1)
        if i >= 2:
            scatter_dp(i - 2)
    chunks = cols // PC
    cut = [chunks * i // 4 for i in range(5)]
    lax.fori_loop(cut[0], cut[1], proto_cols, 0)
    scatter_sub(n_blk - 1)
    if n_blk >= 2:
        scatter_dp(n_blk - 2)
    lax.fori_loop(cut[1], cut[2], proto_cols, 0)
    scatter_dp(n_blk - 1)
    lax.fori_loop(cut[2], cut[4], proto_cols, 0)
    stores = [pltpu.make_async_copy(gproto_ref, gproto_hbm, load_sem.at[5])]
    stores[0].start()
    total = own[...]
    for k in range(1, n_blk):
        zi = near_z[k]
        arrive(z_in.at[zi], rsz_send.at[zi], rsz_recv.at[zi], {"blk": zi})
        total = total + unpack(z_in.at[zi])
    gview_ref[...] = total
    stores.append(pltpu.make_async_copy(gview_ref, gview_hbm, load_sem.at[6]))
    stores[1].start()
    for copy in stores:
        copy.wait()
    for copy in sends:
        copy.wait_send()


def store(gview_ref, gproto_ref, gview_out, gproto_out, held, sem, out_sem):
    rows = gview_ref.shape[0]
    parts = 8
    size = gproto_ref.shape[0] // parts
    spans = [(gview_ref, gview_out, held.at[pl.ds(0, rows)])]
    for i in range(parts):
        at = pl.ds(i * size, size)
        spans.append((gproto_ref.at[at], gproto_out.at[at], held.at[pl.ds(rows + i * size, size)]))
    ins = [pltpu.make_async_copy(a, h, sem.at[i]) for i, (a, b, h) in enumerate(spans)]
    outs = [pltpu.make_async_copy(h, b, out_sem.at[i]) for i, (a, b, h) in enumerate(spans)]
    for copy in ins:
        copy.start()
    for copy, out in zip(ins, outs):
        copy.wait()
        out.start()
    for out in outs:
        out.wait()


def body_direct(view_a, view_b, prototypes, tile_mask, tile_region):
    n_blk = lax.axis_size("blk")
    n_dp = lax.axis_size("dp")
    hit_dev, width = view_a.shape
    plane = 2 * n_dp
    cols = prototypes.shape[0] // plane
    pairs = n_blk * n_dp
    hits = pairs * 2 * hit_dev
    team = n_blk * plane
    slots = n_blk if n_blk <= 4 else 2
    dma = pltpu.SemaphoreType.DMA
    vmem = pl.BlockSpec(memory_space=pltpu.VMEM)
    hbm = pl.BlockSpec(memory_space=pltpu.HBM)
    grads = pl.pallas_call(
        functools.partial(kernel_direct, n_blk, n_dp, hit_dev, cols),
        out_shape=(
            jax.ShapeDtypeStruct((hit_dev, width), F32),
            jax.ShapeDtypeStruct((cols, width), F32),
        ),
        in_specs=[hbm] * 5,
        out_specs=(hbm, hbm),
        scratch_shapes=[
            pltpu.VMEM((hit_dev, width), F32),
            pltpu.VMEM((cols, width), F32),
            pltpu.SMEM(tile_region.shape, jnp.int32),
            pltpu.SMEM(tile_mask.shape, jnp.int32),
            pltpu.VMEM((hit_dev, width), BF16),
            pltpu.VMEM((hit_dev, width), BF16),
            pltpu.VMEM((n_blk, n_dp, 2, hit_dev, width), BF16),
            pltpu.VMEM((n_blk, n_dp, 2, hit_dev, width), BF16),
            pltpu.VMEM((cols, width), BF16),
            pltpu.VMEM((hits, cols), BF16),
            pltpu.VMEM((hits, cols), F32),
            pltpu.VMEM((min(2, n_dp) * 2 * hit_dev, TILE), F32),
            pltpu.VMEM((8, cols), F32),
            pltpu.VMEM((8, cols), F32),
            pltpu.VMEM((pairs, TILE), F32),
            pltpu.VMEM((pairs, TILE), F32),
            pltpu.VMEM((ITERS, team, pairs, TILE), F32),
            pltpu.VMEM((team, pairs, TILE), F32),
            pltpu.VMEM((16, hits), BF16),
            pltpu.VMEM((hits, cols), F32),
            pltpu.VMEM((slots, 2, n_dp, hit_dev, width), F32),
            pltpu.VMEM((slots, hit_dev, width), F32),
            pltpu.VMEM((hit_dev, width), F32),
            pltpu.VMEM((slots, max(n_dp - 1, 1), hit_dev + SCALE_ROWS, width), jnp.int16),
            pltpu.VMEM((n_blk, n_dp, hit_dev, width), F32),
            pltpu.VMEM((n_blk, max(n_dp - 1, 1), hit_dev + SCALE_ROWS, width), jnp.int16),
            pltpu.VMEM((n_blk, hit_dev + SCALE_ROWS, width), jnp.int16),
            pltpu.VMEM((n_blk, hit_dev + SCALE_ROWS, width), jnp.int16),
            dma((7,)),
            dma((2, n_blk)),
            dma((2, n_blk)),
            dma((2, n_blk, n_dp)),
            dma((2, n_blk, n_dp)),
            dma((2, n_blk, n_dp)),
            dma((2, n_blk, n_dp)),
            dma((ITERS, team)),
            dma((ITERS, team)),
            dma((team,)),
            dma((team,)),
            dma((n_blk,)),
            dma((n_blk,)),
            dma((n_blk, n_dp)),
            dma((n_blk, n_dp)),
            dma((n_blk,)),
            dma((n_blk,)),
        ],
        compiler_params=pltpu.CompilerParams(
            collective_id=0, has_side_effects=True, vmem_limit_bytes=(64 << 20)
        ),
    )(tile_region, tile_mask, view_a, view_b, prototypes)
    return pl.pallas_call(
        store,
        out_shape=(
            jax.ShapeDtypeStruct((hit_dev, width), F32),
            jax.ShapeDtypeStruct((cols, width), F32),
        ),
        in_specs=[hbm] * 2,
        out_specs=[hbm] * 2,
        scratch_shapes=[pltpu.VMEM((hit_dev + cols, width), F32), dma((9,)), dma((9,))],
        compiler_params=pltpu.CompilerParams(vmem_limit_bytes=64 << 20),
    )(*grads)


def body(view_a, view_b, prototypes, tile_mask, tile_region):
    n_blk = lax.axis_size("blk")
    n_dp = lax.axis_size("dp")
    hit_dev, width = view_a.shape
    plane = 2 * n_dp
    cols = prototypes.shape[0] // plane
    pairs = n_blk * n_dp
    hits = pairs * 2 * hit_dev
    team = n_blk * plane if n_blk * plane <= 16 else plane
    slots = n_blk if n_blk <= 4 else 2
    dma = pltpu.SemaphoreType.DMA
    vmem = pl.BlockSpec(memory_space=pltpu.VMEM)
    smem = pl.BlockSpec(memory_space=pltpu.SMEM)
    return pl.pallas_call(
        functools.partial(kernel, n_blk, n_dp, hit_dev, cols),
        out_shape=(
            jax.ShapeDtypeStruct((hit_dev, width), F32),
            jax.ShapeDtypeStruct((cols, width), F32),
        ),
        in_specs=[smem, smem, vmem, vmem, pl.BlockSpec(memory_space=pl.ANY)],
        out_specs=(vmem, vmem),
        scratch_shapes=[
            pltpu.VMEM((n_blk, n_dp, 2, hit_dev, width), BF16),
            pltpu.VMEM((n_blk, n_dp, 2, hit_dev, width), BF16),
            pltpu.VMEM((cols, width), BF16),
            pltpu.VMEM((hits, cols), BF16),
            pltpu.VMEM((hits, cols), F32),
            pltpu.VMEM((min(2, n_dp) * 2 * hit_dev, TILE), F32),
            pltpu.VMEM((8, cols), F32),
            pltpu.VMEM((8, cols), F32),
            pltpu.VMEM((pairs, TILE), F32),
            pltpu.VMEM((pairs, TILE), F32),
            pltpu.VMEM((ITERS, team, 2 * pairs, TILE), F32),
            pltpu.VMEM((ITERS, n_blk, 2 * pairs, TILE), F32),
            pltpu.VMEM((slots, 2, n_dp, hit_dev, width), F32),
            pltpu.VMEM((slots, n_dp, hit_dev, width), F32),
            pltpu.VMEM((n_blk, n_dp, hit_dev, width), F32),
            pltpu.VMEM((n_blk, n_dp - 1, hit_dev, width), F32),
            pltpu.VMEM((n_blk, hit_dev, width), F32),
            pltpu.VMEM((n_blk, hit_dev, width), F32),
            dma,
            dma((2, n_blk)),
            dma((2, n_blk)),
            dma((2, n_blk, n_dp)),
            dma((2, n_blk, n_dp)),
            dma((2, n_blk, n_dp)),
            dma((2, n_blk, n_dp)),
            dma((ITERS, team)),
            dma((ITERS, team)),
            dma((ITERS, n_blk)),
            dma((ITERS, n_blk)),
            dma((n_blk,)),
            dma((n_blk,)),
            dma((n_blk, n_dp)),
            dma((n_blk, n_dp)),
            dma((n_blk,)),
            dma((n_blk,)),
        ],
        compiler_params=pltpu.CompilerParams(
            collective_id=0, has_side_effects=True, vmem_limit_bytes=(50 if team > plane else 62) << 20
        ),
    )(tile_region, tile_mask, view_a, view_b, prototypes)


def solution(mesh):
    team = mesh.shape["blk"] * mesh.shape["dp"] * mesh.shape["sub"]
    small = mesh.shape["blk"] >= 3 and team <= 16
    spread = P(("groups", "blk", "dp", "sub"), None)
    return jax.shard_map(
        body_direct if small else body,
        mesh=mesh,
        in_specs=(spread, spread, P("blk", None), P(), P("groups")),
        out_specs=(spread, spread),
        check_vma=False,
    )
```
